32 devices in a mesh: kz: 4 (over x, core), tile: 8 (over z, y).
Axes of the slice: x: 2, y: 2, z: 4, core: 2. Of those that a mesh axis runs over, the one named last changes fastest.
Arguments:
- coil_data: bfloat16 [4, 8, 4, 8, 2, 16, 128], P('kz', 'tile'), may hold values from -6 to 6
- frame_of: int32 [4, 8, 4, 8, 2], P('kz', 'tile'), may hold values from 0 to 999
- basis: bfloat16 [1000, 10], replicated, may hold values from -4 to 4
- sample_pos: float32 [4, 8, 4, 8, 2, 2, 128], P('kz', 'tile'), may hold values from 1.5 to 30.5, as said below
- window_at: int32 [4, 8, 4, 8, 2, 2], P('kz', 'tile'), may hold values from -2 to 639, as said below
- live_count: int32 [4, 8, 4, 8], P('kz', 'tile'), may hold values from 0 to 2, as said below
Outputs:
- image: bfloat16 [4, 640, 102400], P('kz', None, 'tile')
The draws below stay inside these ranges and needn't reach their ends.
Inputs may be any that keep to these rules, and one draw needn't show every extreme that they name: `live_count`: live slots of a pair are its first ones; destination tiles from 3 up to but not including 8 * 5 // 8 receive every slot from every acquiring device. `window_at`: the first entry (row0) lies in -2 to 78, the second (col0) in 0 to 639. `sample_pos`: the first entry lies in 1.5 to 2.5, the second in 1.5 to 32 - 1.5.
All inputs are finite; a program needn't handle non-finite values.
Results may differ from the reference program's by a relative error of at most 0.0077.
Values may be sent and summed in bfloat16 or wider, within the bound.
No kernel may reach another device: no remote copies, remote signals or barrier semaphores. Data moves between devices by JAX's collectives and lax.ppermute only.
A program may use at most 192 MiB of HBM per device.

```python
import math
import jax
import jax.numpy as jnp
from jax import lax

PLANE = 640
RANK = 10
COILS = 8
FRAMES = 1000
BLOCK = 128
SLOTS = 2
WIN_ROWS = 4
WIN_COLS = 32
PARTITIONS = 4
TILES = 8
TILE_ROWS = 80


def draw_sample_pos(key, part):
    shape = (PARTITIONS, TILES, PARTITIONS, TILES, SLOTS, BLOCK)
    key_row, key_col = jax.random.split(key)
    rows = jax.random.uniform(key_row, shape, jnp.float32, 1.5, 2.5)
    cols = jax.random.uniform(key_col, shape, jnp.float32, 1.5, WIN_COLS - 1.5)
    return jnp.stack([rows, cols], axis=5)


def draw_window_at(key, part):
    shape = (PARTITIONS, TILES, PARTITIONS, TILES, SLOTS)
    key_row, key_col = jax.random.split(jax.random.fold_in(key, 7))
    rows = jax.random.randint(key_row, shape, -2, TILE_ROWS - 1)
    cols = jax.random.randint(key_col, shape, 0, PLANE)
    return jnp.stack([rows, cols], axis=5).astype(jnp.int32)


def draw_live_count(key, part):
    shape = (PARTITIONS, TILES, PARTITIONS, TILES)
    base = jax.random.randint(jax.random.fold_in(key, 11), shape, 0, SLOTS + 1)
    tile_idx = jnp.arange(TILES, dtype=jnp.int32)[None, :, None, None]
    hot = (tile_idx >= TILES * 3 // 8) & (tile_idx < TILES * 5 // 8)
    return jnp.where(hot, SLOTS, base).astype(jnp.int32)


def place_ends(values, stream_key, smallest, largest):
    spot = [jax.random.randint(jax.random.fold_in(stream_key, axis), (), 0, length) for axis, length in enumerate(values.shape)]
    widest = values.shape.index(max(values.shape))
    next_to = spot[:widest] + [(spot[widest] + 1) % values.shape[widest]] + spot[widest + 1:]
    return values.at[tuple(spot)].set(smallest).at[tuple(next_to)].set(largest)


def shard_levels(own_key, extent, cuts, smallest, largest):
    factor_of = 1.0
    for position, blocks in cuts:
        steps = jax.random.uniform(jax.random.fold_in(jax.random.fold_in(own_key, 6), position), (blocks,), jnp.float32, smallest / len(cuts), largest / len(cuts))
        factor_of = factor_of * jnp.repeat(jnp.exp(steps), extent[position] // blocks).reshape((-1,) + (1,) * (len(extent) - 1 - position))
    return factor_of


def noise(stream_key, shape, scale, limit, shards=(), held_as=jnp.bfloat16):
    gain = shard_levels(stream_key, shape, shards, -0.22, 0.18) if shards else 1.0
    drawn = jax.random.normal(stream_key, shape, jnp.float32) * scale * gain
    return jnp.minimum(jnp.maximum(drawn, -limit), limit).astype(held_as)


def setup_inputs(seed: int = 0) -> dict:
    key_of = jax.random.split(jax.random.key(seed), 7)
    coil_data = noise(key_of[0], (PARTITIONS, TILES, PARTITIONS, TILES, SLOTS, 2 * COILS, BLOCK), 1.0, 6.0, ((0, 4), (1, 8)))
    frame_of = place_ends(jax.random.randint(key_of[1], (PARTITIONS, TILES, PARTITIONS, TILES, SLOTS), 0, FRAMES), jax.random.fold_in(key_of[1], 1), 0, FRAMES - 1).astype(jnp.int32)
    basis = noise(key_of[2], (FRAMES, RANK), 1.0, 4.0)
    sample_pos = draw_sample_pos(jax.random.fold_in(key_of[6], 71), 0)
    window_at = draw_window_at(jax.random.fold_in(key_of[6], 71), 0)
    live_count = draw_live_count(jax.random.fold_in(key_of[6], 71), 0)
    return {"coil_data": coil_data, "frame_of": frame_of, "basis": basis, "sample_pos": sample_pos, "window_at": window_at, "live_count": live_count}


def taper(dist):
    inner = 1.0 - (dist / 1.5) ** 2
    return jnp.maximum(inner, 0.0) ** 2


def project(blocks, coeffs):
    count = blocks.shape[0]
    coils = blocks.shape[1] // 2
    ranks = coeffs.shape[1]
    samples = blocks.shape[2]
    data = blocks.astype(jnp.float32).reshape(count, 2, 1, coils, samples)
    scale = coeffs.astype(jnp.float32).reshape(count, 1, ranks, 1, 1)
    return (data * scale).reshape(count, 2 * ranks * coils, samples).astype(jnp.bfloat16)


def wide_product(weights, values):
    return jnp.einsum("gwb,gcb->gwc", weights.astype(jnp.float32), values.astype(jnp.float32))


def grid_tile(proj, offsets, corners, alive, tile_rows, plane):
    count, width, samples = proj.shape
    group = 64
    row_cells = jnp.arange(WIN_ROWS, dtype=jnp.float32)
    col_cells = jnp.arange(WIN_COLS, dtype=jnp.float32)
    cells = jnp.arange(WIN_ROWS * WIN_COLS, dtype=jnp.int32)
    cell_row = cells // WIN_COLS
    cell_col = cells % WIN_COLS

    def step(acc, items):
        values, place, corner, living = items
        row_k = taper(row_cells[None, :, None] - place[:, 0:1, :])
        col_k = taper(col_cells[None, :, None] - place[:, 1:2, :])
        weights = (row_k[:, :, None, :] * col_k[:, None, :, :]).reshape(group, WIN_ROWS * WIN_COLS, samples)
        weights = (weights * living[:, None, None]).astype(jnp.bfloat16)
        contrib = wide_product(weights, values)
        rows = corner[:, 0:1] + 2 + cell_row[None, :]
        cols = (corner[:, 1:2] + cell_col[None, :]) % plane
        acc = acc.at[rows.reshape(-1), cols.reshape(-1)].add(contrib.reshape(-1, width))
        return acc, None

    start = jnp.zeros((tile_rows + 4, plane, width), jnp.float32)
    items = (proj.reshape(-1, group, width, samples), offsets.reshape(-1, group, 2, samples),
             corners.reshape(-1, group, 2), alive.reshape(-1, group))
    acc, _ = lax.scan(step, start, items)
    return acc


def tables(n):
    idx = jnp.arange(n, dtype=jnp.int32)
    phase = ((idx[:, None] * idx[None, :]) % n).astype(jnp.float32) * (2.0 * math.pi / n)
    return jnp.cos(phase).astype(jnp.bfloat16), jnp.sin(phase).astype(jnp.bfloat16)


def combine(first, second, half):
    return jnp.concatenate([first[..., :half] - second[..., half:], second[..., :half] + first[..., half:]], axis=-1)


def reference(coil_data, frame_of, basis, sample_pos, window_at, live_count):
    parts = coil_data.shape[0]
    tiles = coil_data.shape[1]
    slots = coil_data.shape[4]
    pair = coil_data.shape[5]
    samples = coil_data.shape[6]
    width = 2 * basis.shape[1] * (pair // 2)
    half = width // 2
    tile_rows = PLANE // tiles
    cos_tab, sin_tab = tables(PLANE)
    slot_idx = jnp.arange(slots, dtype=jnp.int32)

    def one_part(a):
        data_a = lax.dynamic_index_in_dim(coil_data, a, 2, False)
        frames_a = lax.dynamic_index_in_dim(frame_of, a, 2, False)
        pos_a = lax.dynamic_index_in_dim(sample_pos, a, 0, False)
        win_a = lax.dynamic_index_in_dim(window_at, a, 0, False)
        live_a = lax.dynamic_index_in_dim(live_count, a, 0, False)

        def one_tile(total, t):
            blocks = lax.dynamic_index_in_dim(data_a, t, 2, False)
            frames = lax.dynamic_index_in_dim(frames_a, t, 2, False)
            offsets = lax.dynamic_index_in_dim(pos_a, t, 0, False)
            corners = lax.dynamic_index_in_dim(win_a, t, 0, False)
            counts = lax.dynamic_index_in_dim(live_a, t, 0, False)
            proj = project(blocks.reshape(-1, pair, samples), basis[frames.reshape(-1)])
            alive = (slot_idx[None, None, :] < counts[:, :, None]).astype(jnp.float32)
            acc = grid_tile(proj, offsets.reshape(-1, 2, samples), corners.reshape(-1, 2), alive.reshape(-1), tile_rows, PLANE)
            rows = (t * tile_rows - 2 + jnp.arange(tile_rows + 4, dtype=jnp.int32)) % PLANE
            return total.at[rows].add(acc), None

        total, _ = lax.scan(one_tile, jnp.zeros((PLANE, PLANE, width), jnp.float32), jnp.arange(tiles, dtype=jnp.int32))
        grid = total.astype(jnp.bfloat16).astype(jnp.float32)
        first = jnp.einsum("xkq,ky->xyq", grid, cos_tab.astype(jnp.float32))
        second = jnp.einsum("xkq,ky->xyq", grid, sin_tab.astype(jnp.float32))
        mid = combine(first, second, half).astype(jnp.bfloat16).astype(jnp.float32)
        first = jnp.einsum("kyq,kx->xyq", mid, cos_tab.astype(jnp.float32))
        second = jnp.einsum("kyq,kx->xyq", mid, sin_tab.astype(jnp.float32))
        result = (combine(first, second, half) * (1.0 / PLANE)).astype(jnp.bfloat16)
        return result.reshape(PLANE, PLANE * width)

    return lax.map(one_part, jnp.arange(parts, dtype=jnp.int32))
```

```python
import functools
import math

import jax
import jax.numpy as jnp
from jax import lax
from jax.experimental import pallas as pl
from jax.experimental.pallas import tpu as pltpu
from jax.sharding import PartitionSpec as P

PLANE = 640
WIN_ROWS = 4
WIN_COLS = 32
LANES = 128
META_KX = 64
NT_DIMS = (((1,), (1,)), ((), ()))


def taper(dist):
    inner = 1.0 - (dist * (1.0 / 1.5)) ** 2
    return jnp.maximum(inner, 0.0) ** 2


def phase_of(product):
    return (product % PLANE).astype(jnp.float32) * (2.0 * math.pi / PLANE)


def window_kernel(quad, data_ref, pos_ref, alive_ref, out_ref):
    _, pair, samples = data_ref.shape
    cols = lax.broadcasted_iota(jnp.int32, (WIN_COLS, samples), 0).astype(jnp.float32)
    row = lax.broadcasted_iota(jnp.int32, (quad * WIN_ROWS, samples), 0)
    spread = []
    weights = []
    for q in range(quad):
        place = pos_ref[q]
        col_k = taper(cols - place[1:2, :])
        data = data_ref[q].astype(jnp.float32)
        spread.append((col_k[:, None, :] * data[None, :, :]).reshape(WIN_COLS * pair, samples).astype(jnp.bfloat16))
        row_k = taper((row - q * WIN_ROWS).astype(jnp.float32) - place[0:1, :]) * alive_ref[q]
        mine = (row >= q * WIN_ROWS) & (row < (q + 1) * WIN_ROWS)
        weights.append(jnp.where(mine, row_k, 0.0).astype(jnp.bfloat16))
    out_ref[...] = lax.dot_general(
        jnp.concatenate(weights, axis=1), jnp.concatenate(spread, axis=1), NT_DIMS,
        preferred_element_type=jnp.float32,
    ).astype(jnp.bfloat16)


def grid_windows(raw, pos, alive):
    count, pair, samples = raw.shape
    quad = 4
    width = WIN_COLS * pair
    return pl.pallas_call(
        functools.partial(window_kernel, quad),
        grid=(count // quad,),
        in_specs=[
            pl.BlockSpec((quad, pair, samples), lambda s: (s, 0, 0)),
            pl.BlockSpec((quad, 2, samples), lambda s: (s, 0, 0)),
            pl.BlockSpec((quad, 1, samples), lambda s: (s, 0, 0)),
        ],
        out_specs=pl.BlockSpec((quad * WIN_ROWS, width), lambda s: (s, 0)),
        out_shape=jax.ShapeDtypeStruct((count * WIN_ROWS, width), jnp.bfloat16),
        name="grid_windows",
    )(raw, pos, jnp.broadcast_to(alive[:, None, None], (count, 1, samples)))


def columns_kernel(coils, grid_ref, table_ref, turn_ref, out_ref):
    rows, _ = table_ref.shape
    depth = grid_ref.shape[1]
    ys = rows // (2 * coils)
    flat = lax.dot_general(table_ref[...], grid_ref[0], NT_DIMS, preferred_element_type=jnp.float32)
    flat = flat.reshape(ys, 2, coils, depth)
    real, imag = flat[:, 0], flat[:, 1]
    turn_re = turn_ref[0, 0][:, None, :]
    turn_im = turn_ref[0, 1][:, None, :]
    done_re = real * turn_re - imag * turn_im
    done_im = real * turn_im + imag * turn_re
    both = jnp.concatenate([done_re[:, None], done_im[:, None]], axis=1)
    out_ref[0] = both.reshape(rows, depth).astype(jnp.bfloat16)


def transform_columns(grids, table, turns, coils, chunk):
    tiles, depth, width = grids.shape
    rows = table.shape[0]
    ys = rows // (2 * coils)
    per = depth // chunk
    return pl.pallas_call(
        functools.partial(columns_kernel, coils),
        grid=(tiles, per),
        in_specs=[
            pl.BlockSpec((1, chunk, width), lambda t, k: (t, k, 0)),
            pl.BlockSpec((rows, width), lambda t, k: (0, 0)),
            pl.BlockSpec((1, 2, ys, chunk), lambda t, k: (t, 0, 0, k)),
        ],
        out_specs=pl.BlockSpec((1, rows, chunk), lambda t, k: (t, 0, k)),
        out_shape=jax.ShapeDtypeStruct((tiles, rows, depth), jnp.bfloat16),
        compiler_params=pltpu.CompilerParams(vmem_limit_bytes=40 << 20),
        name="transform_columns",
    )(grids, table, turns)


def image_kernel(blocks, ranks, coils, near, ys_step, *refs):
    mids = refs[:near]
    metas = refs[near : 2 * near]
    wave_ref, out_ref, held = refs[2 * near :]
    step = pl.program_id(0)
    rows, depth = mids[0].shape[1:]
    groups = rows // coils

    @pl.when(step < blocks)
    def _():
        lane = lax.broadcasted_iota(jnp.int32, (depth, LANES), 1).astype(jnp.float32)
        base = (step * LANES).astype(jnp.float32)
        hits = [meta[0][:, META_KX : META_KX + 1] - base == lane for meta in metas]
        for pair in range(ranks // 2):
            total = None
            for d in range(near):
                pick = [
                    jnp.where(hits[d], metas[d][0][:, 2 * pair + e : 2 * pair + e + 1], 0.0).astype(jnp.bfloat16)
                    for e in range(2)
                ]
                part = jnp.dot(mids[d][0], jnp.concatenate(pick, axis=1), preferred_element_type=jnp.float32)
                total = part if total is None else total + part
            low = total[:, :LANES].reshape(groups, 1, coils, LANES)
            high = total[:, LANES:].reshape(groups, 1, coils, LANES)
            both = jnp.concatenate([low, high], axis=1).reshape(groups, 2 * coils, LANES)
            held[:, pair, :, pl.ds(pl.multiple_of(step * LANES, LANES), LANES)] = both.astype(jnp.bfloat16)

    @pl.when(step >= blocks)
    def _():
        first = (step - blocks) * (2 * ys_step)
        block = held[pl.ds(first, 2 * ys_step)]
        plane = block.shape[-1]
        block = block.reshape(ys_step, 2, ranks * coils, plane)
        real, imag = block[:, 0:1], block[:, 1:2]
        straight = block.reshape(ys_step * 2 * ranks * coils, plane)
        crossed = jnp.concatenate([-imag, real], axis=1).reshape(ys_step * 2 * ranks * coils, plane)
        total = lax.dot_general(
            wave_ref[...], jnp.concatenate([straight, crossed], axis=1), NT_DIMS,
            preferred_element_type=jnp.float32,
        )
        out_ref[...] = (total * (1.0 / plane)).astype(jnp.bfloat16)


def form_image(mid, meta, wave, ranks, coils, tile_rows):
    tiles, rows, depth = mid.shape
    plane = wave.shape[0]
    blocks = plane // LANES
    firsts = [(b * LANES - 2) // tile_rows for b in range(blocks)]
    lasts = [(b * LANES + LANES + 1) // tile_rows for b in range(blocks)]
    near = max(last - first + 1 for first, last in zip(firsts, lasts))
    ys = rows // (2 * coils)
    ys_step = 4
    columns = ys_step * 2 * ranks * coils

    def tile_at(d):
        def at(s):
            b = jnp.minimum(s, blocks - 1)
            return ((b * LANES - 2 + tiles * tile_rows) // tile_rows + d) % tiles

        return at

    mid_specs = [pl.BlockSpec((1, rows, depth), lambda s, at=tile_at(d): (at(s), 0, 0)) for d in range(near)]
    meta_specs = [pl.BlockSpec((1, depth, LANES), lambda s, at=tile_at(d): (at(s), 0, 0)) for d in range(near)]
    return pl.pallas_call(
        functools.partial(image_kernel, blocks, ranks, coils, near, ys_step),
        grid=(blocks + ys // ys_step,),
        in_specs=[*mid_specs, *meta_specs, pl.BlockSpec((plane, 2 * plane), lambda s: (0, 0))],
        out_specs=pl.BlockSpec((plane, columns), lambda s: (0, jnp.maximum(s - blocks, 0))),
        out_shape=jax.ShapeDtypeStruct((plane, ys * 2 * ranks * coils), jnp.bfloat16),
        scratch_shapes=[pltpu.VMEM((rows // coils, ranks // 2, 2 * coils, plane), jnp.bfloat16)],
        compiler_params=pltpu.CompilerParams(vmem_limit_bytes=60 << 20),
        name="form_image",
    )(*([mid] * near), *([meta] * near), wave)


def body(coil_data, frame_of, basis, sample_pos, window_at, live_count):
    parts = coil_data.shape[2]
    tiles = coil_data.shape[3]
    slots = coil_data.shape[4]
    pair = coil_data.shape[5]
    samples = coil_data.shape[6]
    coils = pair // 2
    ranks = basis.shape[1]
    tile_rows = PLANE // tiles
    devices = parts * tiles
    count = devices * slots
    depth = count * WIN_ROWS
    my_part = lax.axis_index("kz")
    my_tile = lax.axis_index("tile")
    every = ("kz", "tile")

    raw = lax.all_to_all(
        coil_data.reshape(devices, slots * pair, samples), every, split_axis=0, concat_axis=0, tiled=True
    )
    counts = live_count.reshape(devices)
    slot_idx = jnp.arange(slots, dtype=jnp.int32)
    alive = (slot_idx[None, :] < counts[:, None]).astype(jnp.float32).reshape(count)
    windows = grid_windows(raw.reshape(count, pair, samples), sample_pos.reshape(count, 2, samples), alive)
    grids = lax.all_gather(windows, "tile", axis=0, tiled=False)

    notes = jnp.concatenate([frame_of.reshape(-1), window_at.reshape(-1)])
    notes = lax.all_gather(notes, every, axis=0, tiled=False)
    frames = notes[:, :count].reshape(devices, parts, tiles, slots)
    frames = lax.dynamic_index_in_dim(frames, my_part, 1, False)
    frames = jnp.transpose(frames, (1, 0, 2)).reshape(tiles, count)
    corners = lax.dynamic_slice_in_dim(notes[:, count:].reshape(parts, tiles, count, 2), my_part, 1, 0)[0]
    tile_idx = jnp.arange(tiles, dtype=jnp.int32)
    win_row = jnp.arange(WIN_ROWS, dtype=jnp.int32)
    kx = (tile_idx[:, None, None] * tile_rows + corners[:, :, 0:1] + win_row + PLANE) % PLANE
    kx = kx.reshape(tiles, depth, 1).astype(jnp.float32)
    coeff = jnp.repeat(basis[frames].astype(jnp.float32), WIN_ROWS, axis=1)
    meta = jnp.concatenate(
        [
            jnp.pad(coeff, ((0, 0), (0, 0), (0, META_KX - ranks))),
            jnp.pad(kx, ((0, 0), (0, 0), (0, LANES - META_KX - 1))),
        ],
        axis=2,
    )

    ys = PLANE // tiles
    y = my_tile * ys + jnp.arange(ys, dtype=jnp.int32)
    col0 = jnp.repeat(corners[:, :, 1], WIN_ROWS, axis=1)
    turn = phase_of(col0[:, None, :] * y[None, :, None])
    turns = jnp.stack([jnp.cos(turn), jnp.sin(turn)], axis=1)
    part = jnp.arange(2, dtype=jnp.int32)
    coil = jnp.arange(coils, dtype=jnp.int32)
    win_col = jnp.arange(WIN_COLS, dtype=jnp.int32)
    angle = phase_of(y[:, None] * win_col[None, :])
    cos_y, sin_y = jnp.cos(angle), jnp.sin(angle)
    mix = jnp.stack([jnp.stack([cos_y, -sin_y], axis=-1), jnp.stack([sin_y, cos_y], axis=-1)], axis=1)
    same = (coil[:, None] == coil[None, :]).astype(jnp.float32)
    table = mix[:, :, None, :, :, None] * same[None, None, :, None, None, :]
    table = table.reshape(ys * 2 * coils, WIN_COLS * pair).astype(jnp.bfloat16)
    index = jnp.arange(PLANE, dtype=jnp.int32)
    angle = phase_of(index[:, None] * index[None, :])
    wave = jnp.concatenate([jnp.cos(angle), jnp.sin(angle)], axis=1).astype(jnp.bfloat16)

    mid = transform_columns(grids, table, turns, coils, min(depth, 256))
    image = form_image(mid, meta, wave, ranks, coils, tile_rows)
    return image[None]


def solution(mesh):
    return jax.shard_map(
        body,
        mesh=mesh,
        in_specs=(
            P("kz", "tile", None, None, None, None, None),
            P("kz", "tile", None, None, None),
            P(),
            P("kz", "tile", None, None, None, None, None),
            P("kz", "tile", None, None, None, None),
            P("kz", "tile", None, None),
        ),
        out_specs=P("kz", None, "tile"),
        check_vma=False,
    )
```

```python
import functools
import math

import jax
import jax.numpy as jnp
import numpy as np
from jax import lax
from jax.experimental import pallas as pl
from jax.experimental.pallas import tpu as pltpu
from jax.sharding import PartitionSpec as P

PLANE = 640
WIN_ROWS = 4
WIN_COLS = 32
LANES = 128
NOTES = 16
ROW_NOTE = 13
COL_HIGH = 14
COL_LOW = 15
COL_STEP = 32
FAR_OFF = -1000.0
CHUNK = 256
NT_DIMS = (((1,), (1,)), ((), ()))


def taper(dist):
    inner = 1.0 - (dist / 1.5) ** 2
    return jnp.maximum(inner, 0.0) ** 2


def wave_tables():
    idx = np.arange(PLANE)
    phase = (idx[:, None] * idx[None, :] % PLANE) * (2.0 * math.pi / PLANE)
    return np.cos(phase).astype(jnp.bfloat16), np.sin(phase).astype(jnp.bfloat16)


def dot_nt(left, right):
    return lax.dot_general(left, right, NT_DIMS, preferred_element_type=jnp.float32)


def same_part(shape, row_step, lane_step, lane_shift=0):
    rows = lax.broadcasted_iota(jnp.int32, shape, 0) // row_step
    lanes = lax.broadcasted_iota(jnp.int32, shape, 1) // lane_step + lane_shift
    return (rows == lanes).astype(jnp.float32).astype(jnp.bfloat16)


def table_kernel(coils, wave_ref, out_ref):
    ys = wave_ref.shape[0]
    plane = wave_ref.shape[1] // 2
    rows, width = out_ref.shape
    pick = same_part((LANES, width), 1, 2 * coils)
    cos_y = jnp.dot(wave_ref[:, :LANES], pick, preferred_element_type=jnp.float32)
    sin_y = jnp.dot(wave_ref[:, plane : plane + LANES], pick, preferred_element_type=jnp.float32)
    lane = lax.broadcasted_iota(jnp.int32, (ys, width), 1) % (2 * coils)
    into_re = jnp.where(lane < coils, cos_y, -sin_y)
    into_im = jnp.where(lane < coils, sin_y, cos_y)
    both = jnp.concatenate([into_re[:, None, None, :], into_im[:, None, None, :]], axis=1)
    both = jnp.broadcast_to(both, (ys, 2, coils, width))
    mine = lax.broadcasted_iota(jnp.int32, both.shape, 2)
    other = lax.broadcasted_iota(jnp.int32, both.shape, 3) % coils
    out_ref[...] = jnp.where(mine == other, both, 0.0).reshape(rows, width).astype(jnp.bfloat16)


def column_table(wave_rows, coils):
    ys = wave_rows.shape[0]
    return pl.pallas_call(
        functools.partial(table_kernel, coils),
        out_shape=jax.ShapeDtypeStruct((ys * 2 * coils, WIN_COLS * 2 * coils), jnp.bfloat16),
        compiler_params=pltpu.CompilerParams(vmem_limit_bytes=40 << 20),
        name="column_table",
    )(wave_rows)


def window_kernel(slots, pair, data_ref, rate_ref, pos_ref, place_ref, out_ref):
    sources, _, samples = data_ref.shape
    quad = sources * slots
    step = pl.program_id(0)
    cols = lax.broadcasted_iota(jnp.int32, (WIN_COLS, samples), 0).astype(jnp.float32)
    row = lax.broadcasted_iota(jnp.int32, (quad * WIN_ROWS, samples), 0)
    spread = []
    weights = []
    for q in range(quad):
        place = pos_ref[q]
        col_k = taper(cols - place[1:2, :])
        data = data_ref[q // slots, (q % slots) * pair : (q % slots + 1) * pair].astype(jnp.float32)
        spread.append((col_k[:, None, :] * data[None, :, :]).reshape(WIN_COLS * pair, samples).astype(jnp.bfloat16))
        row_k = taper((row - q * WIN_ROWS).astype(jnp.float32) - place[0:1, :])
        mine = (row >= q * WIN_ROWS) & (row < (q + 1) * WIN_ROWS)
        weights.append(jnp.where(mine, row_k, 0.0).astype(jnp.bfloat16))
    total = dot_nt(jnp.concatenate(weights, axis=1), jnp.concatenate(spread, axis=1))
    size = quad * WIN_ROWS
    out_ref[pl.ds(pl.multiple_of(step * size, size), size), :] = total.astype(jnp.bfloat16)

    @pl.when(step == pl.num_programs(0) - 1)
    def _():
        depth = place_ref.shape[1]
        width = out_ref.shape[1]
        rates = rate_ref[...].astype(jnp.float32).reshape(depth, LANES).astype(jnp.bfloat16)
        notes = dot_nt(same_part((NOTES, LANES), 1, 1), rates) + place_ref[...]
        lanes = min(depth, width)
        for part in range(depth // lanes):
            rows = notes[:, part * lanes : (part + 1) * lanes]
            if lanes < width:
                rows = jnp.concatenate([rows, jnp.zeros((NOTES, width - lanes), jnp.float32)], axis=1)
            out_ref[depth + part * NOTES : depth + (part + 1) * NOTES, :] = rows.astype(jnp.bfloat16)


def grid_windows(raw, pos, place, slots, pair):
    devices, _, samples = raw.shape
    depth = devices * slots * WIN_ROWS
    width = WIN_COLS * pair
    sources = max(1, 4 // slots)
    rate_rows = slots * WIN_ROWS
    total_rows = depth + NOTES * (depth // min(depth, width))
    return pl.pallas_call(
        functools.partial(window_kernel, slots, pair),
        grid=(devices // sources,),
        in_specs=[
            pl.BlockSpec((sources, slots * pair, samples), lambda s: (s, 0, 0)),
            pl.BlockSpec((devices, rate_rows, samples), lambda s: (0, slots * pair // rate_rows, 0)),
            pl.BlockSpec((sources * slots, 2, samples), lambda s: (s, 0, 0)),
            pl.BlockSpec((NOTES, depth), lambda s: (0, 0)),
        ],
        out_specs=pl.BlockSpec((total_rows, width), lambda s: (0, 0)),
        out_shape=jax.ShapeDtypeStruct((total_rows, width), jnp.bfloat16),
        name="grid_windows",
    )(raw, raw, pos, place)


def columns_kernel(coils, odd_ref, mine_ref, mine_notes, other_ref, other_notes, table_ref, wave_ref, out_ref, notes_ref):
    rows = table_ref.shape[0]
    ys = rows // (2 * coils)
    plane = wave_ref.shape[1] // 2
    depth = mine_ref.shape[0]
    take_mine = odd_ref[0] == pl.program_id(0)
    grids = jnp.where(take_mine, mine_ref[...], other_ref[...])
    notes = jnp.where(take_mine, mine_notes[...], other_notes[...])
    notes_ref[0] = notes
    notes = notes.astype(jnp.float32)
    col0 = notes[COL_HIGH : COL_HIGH + 1] * COL_STEP + notes[COL_LOW : COL_LOW + 1]
    row = lax.broadcasted_iota(jnp.int32, (plane, depth), 0).astype(jnp.float32)
    corner = (row == col0).astype(jnp.float32).astype(jnp.bfloat16)
    turn_re = jnp.dot(wave_ref[:, :plane], corner, preferred_element_type=jnp.float32)[:, None, :]
    turn_im = jnp.dot(wave_ref[:, plane:], corner, preferred_element_type=jnp.float32)[:, None, :]
    flat = dot_nt(table_ref[...], grids).reshape(ys, 2, coils, depth)
    real, imag = flat[:, 0], flat[:, 1]
    done_re = real * turn_re - imag * turn_im
    done_im = real * turn_im + imag * turn_re
    both = jnp.concatenate([done_re[:, None], done_im[:, None]], axis=1)
    out_ref[0] = both.reshape(rows, depth).astype(jnp.bfloat16)


def transform_columns(odd, mine, other, table, wave_rows, depth, coils):
    width = mine.shape[1]
    rows = table.shape[0]
    ys, waves = wave_rows.shape
    chunk = min(depth, CHUNK)
    per = depth // chunk
    grid_spec = pl.BlockSpec((chunk, width), lambda e, k: (k, 0))
    note_spec = pl.BlockSpec(
        (NOTES, chunk), lambda e, k: (depth // NOTES + k * chunk // width, k * chunk % width // chunk)
    )
    return pl.pallas_call(
        functools.partial(columns_kernel, coils),
        grid=(2, per),
        in_specs=[
            pl.BlockSpec(memory_space=pltpu.SMEM),
            grid_spec,
            note_spec,
            grid_spec,
            note_spec,
            pl.BlockSpec((rows, width), lambda e, k: (0, 0)),
            pl.BlockSpec((ys, waves), lambda e, k: (0, 0)),
        ],
        out_specs=[
            pl.BlockSpec((1, rows, chunk), lambda e, k: (e, 0, k)),
            pl.BlockSpec((1, NOTES, chunk), lambda e, k: (e, 0, k)),
        ],
        out_shape=[
            jax.ShapeDtypeStruct((2, rows, depth), jnp.bfloat16),
            jax.ShapeDtypeStruct((2, NOTES, depth), jnp.bfloat16),
        ],
        compiler_params=pltpu.CompilerParams(vmem_limit_bytes=40 << 20),
        cost_estimate=pl.CostEstimate(
            flops=2 * 2 * rows * width * depth, bytes_accessed=2 * 2 * rows * depth, transcendentals=0
        ),
        name="transform_columns",
    )(odd, mine, mine, other, other, table, wave_rows)


def rows_kernel(bases, ranks, coils, *refs):
    near = len(bases)
    mids = refs[:near]
    notes = refs[near : 2 * near]
    out_ref = refs[2 * near]
    held = refs[2 * near + 1] if len(refs) > 2 * near + 1 else None
    _, rows, chunk = mids[0].shape
    groups = rows // coils
    step = pl.program_id(0)
    left = jnp.concatenate([mid[0] for mid in mids], axis=1)
    sub = lax.broadcasted_iota(jnp.int32, (LANES, chunk), 0).astype(jnp.float32)
    told = [note[0].astype(jnp.float32) for note in notes]
    hits = [told[d][ROW_NOTE : ROW_NOTE + 1] + bases[d] == sub for d in range(near)]

    def finish(pair, total):
        low = total[:, :LANES].reshape(groups, 1, coils, LANES)
        high = total[:, LANES:].reshape(groups, 1, coils, LANES)
        both = jnp.concatenate([low, high], axis=1).reshape(groups, 2 * coils, LANES)
        out_ref[:, pair] = both.astype(jnp.bfloat16)

    for pair in range(ranks // 2):
        right = jnp.concatenate(
            [
                jnp.concatenate(
                    [jnp.where(hits[d], told[d][rank : rank + 1], 0.0).astype(jnp.bfloat16) for d in range(near)], axis=1
                )
                for rank in (2 * pair, 2 * pair + 1)
            ],
            axis=0,
        )
        total = dot_nt(left, right)
        if held is None:
            finish(pair, total)
        else:

            @pl.when(step == 0)
            def _(pair=pair, total=total):
                held[pair] = total

            @pl.when(step > 0)
            def _(pair=pair, total=total):
                held[pair] += total

            @pl.when(step == pl.num_programs(0) - 1)
            def _(pair=pair):
                finish(pair, held[pair])


def expand_rows(mids, notes, picks, bases, ranks, coils):
    _, rows, depth = mids[0].shape
    near = len(mids)
    chunk = min(depth, CHUNK)
    per = depth // chunk
    groups = rows // coils
    shape = (groups, ranks // 2, 2 * coils, LANES)
    return pl.pallas_call(
        functools.partial(rows_kernel, bases, ranks, coils),
        grid=(per,),
        in_specs=[
            *(pl.BlockSpec((1, rows, chunk), lambda k, e=e: (e, 0, k)) for e in picks),
            *(pl.BlockSpec((1, NOTES, chunk), lambda k, e=e: (e, 0, k)) for e in picks),
        ],
        out_specs=pl.BlockSpec(shape, lambda k: (0, 0, 0, 0)),
        out_shape=jax.ShapeDtypeStruct(shape, jnp.bfloat16),
        scratch_shapes=[pltpu.VMEM((ranks // 2, rows, 2 * LANES), jnp.float32)] if per > 1 else [],
        compiler_params=pltpu.CompilerParams(vmem_limit_bytes=50 << 20),
        cost_estimate=pl.CostEstimate(
            flops=2 * rows * near * depth * ranks * LANES, bytes_accessed=2 * rows * ranks * LANES, transcendentals=0
        ),
        name="expand_rows",
    )(*mids, *notes)


def image_kernel(*refs):
    wave_ref, out_ref = refs[-2:]
    plane = out_ref.shape[0]
    block = jnp.concatenate([ref[...] for ref in refs[:-2]], axis=-1)
    groups, pairs, inner, _ = block.shape
    block = block.reshape(groups // 2, 2, pairs * inner, plane)
    real, imag = block[:, 0:1], block[:, 1:2]
    columns = groups * pairs * inner
    straight = block.reshape(columns, plane)
    crossed = jnp.concatenate([-imag, real], axis=1).reshape(columns, plane)
    total = dot_nt(wave_ref[...], jnp.concatenate([straight, crossed], axis=1))
    out_ref[...] = (total * (1.0 / plane)).astype(jnp.bfloat16)


def form_image(blocks, wave):
    plane = wave.shape[0]
    groups, pairs, inner, _ = blocks[0].shape
    step = 8
    columns = step * pairs * inner
    return pl.pallas_call(
        image_kernel,
        grid=(groups // step,),
        in_specs=[
            *(pl.BlockSpec((step, pairs, inner, LANES), lambda s: (s, 0, 0, 0)) for _ in blocks),
            pl.BlockSpec((plane, 2 * plane), lambda s: (0, 0)),
        ],
        out_specs=pl.BlockSpec((plane, columns), lambda s: (0, s)),
        out_shape=jax.ShapeDtypeStruct((plane, groups * pairs * inner), jnp.bfloat16),
        compiler_params=pltpu.CompilerParams(vmem_limit_bytes=40 << 20),
        cost_estimate=pl.CostEstimate(
            flops=4 * plane * plane * groups * pairs * inner,
            bytes_accessed=4 * plane * groups * pairs * inner,
            transcendentals=0,
        ),
        name="form_image",
    )(*blocks, wave)


def from_tiles(value, source_of):
    count = lax.axis_size("tile")
    return lax.ppermute(value, "tile", [(source_of(t), t) for t in range(count)])


def body(coil_data, frame_of, basis, sample_pos, window_at, live_count):
    parts = coil_data.shape[2]
    tiles = coil_data.shape[3]
    slots = coil_data.shape[4]
    pair = coil_data.shape[5]
    samples = coil_data.shape[6]
    coils = pair // 2
    ranks = basis.shape[1]
    tile_rows = PLANE // tiles
    devices = parts * tiles
    count = devices * slots
    depth = count * WIN_ROWS
    ys = PLANE // tiles
    my_tile = lax.axis_index("tile")
    odd = my_tile % 2

    rates = jnp.broadcast_to(basis[frame_of.reshape(devices, slots)][:, :, None, :], (devices, slots, WIN_ROWS, ranks))
    rates = jnp.pad(rates.reshape(devices, slots * WIN_ROWS, ranks), ((0, 0), (0, 0), (0, samples - ranks)))
    packed = jnp.concatenate([coil_data.reshape(devices, slots * pair, samples), rates], axis=1)
    raw = lax.all_to_all(packed, ("kz", "tile"), split_axis=0, concat_axis=0, tiled=True)

    counts = live_count.reshape(devices)
    slot_idx = jnp.arange(slots, dtype=jnp.int32)
    alive = (slot_idx[None, :] < counts[:, None]).reshape(count, 1, 1)
    pos = jnp.where(alive, sample_pos.reshape(count, 2, samples), FAR_OFF)
    corners = window_at.reshape(count, 2)
    win_row = jnp.arange(WIN_ROWS, dtype=jnp.int32)
    from_row = (odd * tile_rows + 2 + corners[:, 0:1] + win_row).reshape(1, depth)
    col0 = jnp.repeat(corners[:, 1], WIN_ROWS).reshape(1, depth)
    place = jnp.concatenate([from_row, col0 // COL_STEP, col0 % COL_STEP], axis=0).astype(jnp.float32)
    place = jnp.pad(place, ((ROW_NOTE, NOTES - ROW_NOTE - 3), (0, 0)))

    cos_tab, sin_tab = wave_tables()
    wave = lax.optimization_barrier(jnp.asarray(np.concatenate([cos_tab, sin_tab], axis=1)))
    wave_rows = lax.dynamic_slice_in_dim(wave, my_tile * ys, ys, 0)
    table = column_table(wave_rows, coils)
    turned = (my_tile // 2) * (2 * tile_rows)
    rolled = [
        lax.dynamic_slice_in_dim(jnp.concatenate([tab, tab], axis=1), turned, PLANE, 1)
        for tab in (wave[:, :PLANE], wave[:, PLANE:])
    ]
    wave_turned = jnp.concatenate(rolled, axis=1)

    windows = grid_windows(raw, pos, place, slots, pair)

    pairs = tiles // 2
    mine = [windows]
    for shift in range(1, pairs):
        mine.append(from_tiles(windows, lambda t, shift=shift: (t // 2 + shift) % pairs * 2 + t % 2))
    other = [from_tiles(block, lambda t: t // 2 * 2 + 1 - t % 2) for block in mine]
    odd_ref = odd.astype(jnp.int32).reshape(1)
    mids, notes = zip(
        *(transform_columns(odd_ref, a, b, table, wave_rows, depth, coils) for a, b in zip(mine, other))
    )

    blocks = []
    for b in range(PLANE // LANES):
        first = (b * LANES - 2) // tile_rows
        last = (b * LANES + LANES + 1) // tile_rows
        at = range(first, last + 1)
        groups = [t % tiles // 2 for t in at]
        picks = [t % 2 for t in at]
        bases = [float(t // 2 * 2 * tile_rows - 2 - b * LANES) for t in at]
        blocks.append(expand_rows([mids[g] for g in groups], [notes[g] for g in groups], picks, bases, ranks, coils))
    return form_image(blocks, wave_turned)[None]


def solution(mesh):
    return jax.shard_map(
        body,
        mesh=mesh,
        in_specs=(
            P("kz", "tile", None, None, None, None, None),
            P("kz", "tile", None, None, None),
            P(),
            P("kz", "tile", None, None, None, None, None),
            P("kz", "tile", None, None, None, None),
            P("kz", "tile", None, None),
        ),
        out_specs=P("kz", None, "tile"),
        check_vma=False,
    )
```

```python
import functools
import math

import jax
import jax.numpy as jnp
import numpy as np
from jax import lax
from jax.experimental import pallas as pl
from jax.experimental.pallas import tpu as pltpu
from jax.sharding import PartitionSpec as P

PLANE = 640
WIN_ROWS = 4
WIN_COLS = 32
LANES = 128
NOTES = 16
ROW_NOTE = 13
COL_HIGH = 14
COL_LOW = 15
COL_STEP = 32
FAR_OFF = -1000.0
CHUNK = 256
NT_DIMS = (((1,), (1,)), ((), ()))


def taper(dist):
    inner = 1.0 - (dist / 1.5) ** 2
    return jnp.maximum(inner, 0.0) ** 2


def wave_tables():
    idx = np.arange(PLANE)
    phase = (idx[:, None] * idx[None, :] % PLANE) * (2.0 * math.pi / PLANE)
    return np.cos(phase).astype(jnp.bfloat16), np.sin(phase).astype(jnp.bfloat16)


def dot_nt(left, right):
    return lax.dot_general(left, right, NT_DIMS, preferred_element_type=jnp.float32)


def unit(shape, dtype=jnp.bfloat16):
    return (lax.broadcasted_iota(jnp.int32, shape, 0) == lax.broadcasted_iota(jnp.int32, shape, 1)).astype(jnp.float32).astype(dtype)


def table_kernel(coils, wave_ref, rows_ref, lanes_ref, out_ref, waves_ref):
    ys = rows_ref.shape[0]
    plane = wave_ref.shape[0]
    rows, width = out_ref.shape
    spot = lax.broadcasted_iota(jnp.int32, (LANES, width), 0)
    lane = lax.broadcasted_iota(jnp.int32, (LANES, width), 1)
    pick = (spot == lane % WIN_COLS).astype(jnp.float32).astype(jnp.bfloat16)
    cos_y = jnp.dot(rows_ref[:, :LANES], pick, preferred_element_type=jnp.float32)
    sin_y = jnp.dot(rows_ref[:, plane : plane + LANES], pick, preferred_element_type=jnp.float32)
    lane = lax.broadcasted_iota(jnp.int32, (ys, width), 1) // WIN_COLS
    into_re = jnp.where(lane < coils, cos_y, -sin_y)
    into_im = jnp.where(lane < coils, sin_y, cos_y)
    both = jnp.concatenate([into_re[:, None, None, :], into_im[:, None, None, :]], axis=1)
    both = jnp.broadcast_to(both, (ys, 2, coils, width))
    mine = lax.broadcasted_iota(jnp.int32, both.shape, 2)
    other = lax.broadcasted_iota(jnp.int32, both.shape, 3) // WIN_COLS % coils
    out_ref[...] = jnp.where(mine == other, both, 0.0).reshape(rows, width).astype(jnp.bfloat16)

    half, double = waves_ref.shape[1:]
    held = double // 2
    row = lax.broadcasted_iota(jnp.int32, (plane, held), 0)
    for parity in range(2):
        pick = (row == lanes_ref[parity : parity + 1, :]).astype(jnp.float32).astype(jnp.bfloat16)
        for part in range(2):
            waves_ref[parity, :, part * held : (part + 1) * held] = jnp.dot(
                wave_ref[:half, part * plane : (part + 1) * plane], pick, preferred_element_type=jnp.float32
            ).astype(jnp.bfloat16)


def make_tables(wave, wave_rows, lane_rows, coils):
    ys = wave_rows.shape[0]
    plane = wave.shape[0]
    return pl.pallas_call(
        functools.partial(table_kernel, coils),
        out_shape=[
            jax.ShapeDtypeStruct((ys * 2 * coils, WIN_COLS * 2 * coils), jnp.bfloat16),
            jax.ShapeDtypeStruct((2, plane // 2, 2 * lane_rows.shape[1]), jnp.bfloat16),
        ],
        compiler_params=pltpu.CompilerParams(vmem_limit_bytes=40 << 20),
        name="make_tables",
    )(wave, wave_rows, lane_rows)


def window_kernel(slots, pair, data_ref, rate_ref, weight_ref, place_ref, out_ref, held, rates):
    sources = data_ref.shape[0]
    count = held.shape[0] // pair
    step = pl.program_id(0)
    for q in range(sources * slots):
        data = data_ref[q // slots, (q % slots) * pair : (q % slots + 1) * pair]
        first = (step * sources * slots + q) * pair
        held[pl.ds(pl.multiple_of(first, pair), pair), :] = dot_nt(data, weight_ref[q])

    @pl.when(step == pl.num_programs(0) - 1)
    def _():
        depth = place_ref.shape[1]
        width = out_ref.shape[1]
        per = LANES // WIN_COLS
        lane = lax.broadcasted_iota(jnp.int32, (count, LANES), 1) // WIN_COLS
        for group in range(pair // per):
            rows = [held[pl.ds(group * per + q, count, stride=pair), :] for q in range(per)]
            for i in range(WIN_ROWS):
                total = None
                for q in range(per):
                    turn = (q - i) % per * WIN_COLS
                    moved = pltpu.roll(rows[q], turn, 1) if turn else rows[q]
                    total = moved if total is None else jnp.where(lane == q, moved, total)
                out_ref[i * count : (i + 1) * count, group * LANES : (group + 1) * LANES] = total.astype(jnp.bfloat16)
        rates[...] = rate_ref[...].astype(jnp.float32).reshape(rates.shape)
        once = rates[pl.ds(0, count, stride=WIN_ROWS), :].astype(jnp.bfloat16)
        notes = dot_nt(unit((NOTES, LANES)), jnp.concatenate([once] * WIN_ROWS, axis=0)) + place_ref[...]
        lanes = min(depth, width)
        for part in range(depth // lanes):
            part_rows = notes[:, part * lanes : (part + 1) * lanes]
            if lanes < width:
                part_rows = jnp.concatenate([part_rows, jnp.zeros((NOTES, width - lanes), jnp.float32)], axis=1)
            out_ref[depth + part * NOTES : depth + (part + 1) * NOTES, :] = part_rows.astype(jnp.bfloat16)


def grid_windows(raw, weights, place, slots, pair):
    devices, _, samples = raw.shape
    count = devices * slots
    depth = count * WIN_ROWS
    width = WIN_COLS * pair
    sources = 8
    rate_rows = slots * WIN_ROWS
    total_rows = depth + NOTES * (depth // min(depth, width))
    return pl.pallas_call(
        functools.partial(window_kernel, slots, pair),
        grid=(devices // sources,),
        in_specs=[
            pl.BlockSpec((sources, slots * pair, samples), lambda s: (s, 0, 0)),
            pl.BlockSpec((devices, rate_rows, samples), lambda s: (0, slots * pair // rate_rows, 0)),
            pl.BlockSpec((sources * slots, LANES, samples), lambda s: (s, 0, 0)),
            pl.BlockSpec((NOTES, depth), lambda s: (0, 0)),
        ],
        out_specs=pl.BlockSpec((total_rows, width), lambda s: (0, 0)),
        out_shape=jax.ShapeDtypeStruct((total_rows, width), jnp.bfloat16),
        scratch_shapes=[
            pltpu.VMEM((count * pair, LANES), jnp.float32),
            pltpu.VMEM((devices * rate_rows, LANES), jnp.float32),
        ],
        compiler_params=pltpu.CompilerParams(vmem_limit_bytes=24 << 20),
        name="grid_windows",
    )(raw, raw, weights, place)


def columns_kernel(coils, odd_ref, mine_ref, mine_notes, other_ref, other_notes, table_ref, wave_ref, out_ref, notes_ref):
    rows = table_ref.shape[0]
    ys = rows // (2 * coils)
    plane = wave_ref.shape[1] // 2
    depth = mine_ref.shape[0]
    take_mine = odd_ref[0] == pl.program_id(0)
    grids = jnp.where(take_mine, mine_ref[...], other_ref[...])
    notes = jnp.where(take_mine, mine_notes[...], other_notes[...])
    notes_ref[0] = notes
    notes = notes.astype(jnp.float32)
    col0 = notes[COL_HIGH : COL_HIGH + 1] * COL_STEP + notes[COL_LOW : COL_LOW + 1]
    row = lax.broadcasted_iota(jnp.int32, (plane, depth), 0).astype(jnp.float32)
    corner = (row == col0).astype(jnp.float32).astype(jnp.bfloat16)
    turn_re = jnp.dot(wave_ref[:, :plane], corner, preferred_element_type=jnp.float32)[:, None, :]
    turn_im = jnp.dot(wave_ref[:, plane:], corner, preferred_element_type=jnp.float32)[:, None, :]
    flat = dot_nt(table_ref[...], grids).reshape(ys, 2, coils, depth)
    real, imag = flat[:, 0], flat[:, 1]
    done_re = real * turn_re - imag * turn_im
    done_im = real * turn_im + imag * turn_re
    both = jnp.concatenate([done_re[:, None], done_im[:, None]], axis=1)
    out_ref[0] = both.reshape(rows, depth).astype(jnp.bfloat16)


def transform_columns(odd, mine, other, table, wave_rows, depth, coils):
    width = mine.shape[1]
    rows = table.shape[0]
    ys, waves = wave_rows.shape
    chunk = min(depth, CHUNK)
    per = depth // chunk
    grid_spec = pl.BlockSpec((chunk, width), lambda e, k: (k, 0))
    note_spec = pl.BlockSpec(
        (NOTES, chunk), lambda e, k: (depth // NOTES + k * chunk // width, k * chunk % width // chunk)
    )
    return pl.pallas_call(
        functools.partial(columns_kernel, coils),
        grid=(2, per),
        in_specs=[
            pl.BlockSpec(memory_space=pltpu.SMEM),
            grid_spec,
            note_spec,
            grid_spec,
            note_spec,
            pl.BlockSpec((rows, width), lambda e, k: (0, 0)),
            pl.BlockSpec((ys, waves), lambda e, k: (0, 0)),
        ],
        out_specs=[
            pl.BlockSpec((1, rows, chunk), lambda e, k: (e, 0, k)),
            pl.BlockSpec((1, NOTES, chunk), lambda e, k: (e, 0, k)),
        ],
        out_shape=[
            jax.ShapeDtypeStruct((2, rows, depth), jnp.bfloat16),
            jax.ShapeDtypeStruct((2, NOTES, depth), jnp.bfloat16),
        ],
        compiler_params=pltpu.CompilerParams(vmem_limit_bytes=28 << 20),
        cost_estimate=pl.CostEstimate(
            flops=2 * 2 * rows * width * depth, bytes_accessed=2 * 2 * rows * depth, transcendentals=0
        ),
        name="transform_columns",
    )(odd, mine, mine, other, other, table, wave_rows)


def rows_kernel(seats, second, ranks, coils, *refs):
    near = len(seats)
    mids = refs[:near]
    notes = refs[near : 2 * near]
    out_ref = refs[2 * near]
    held = refs[2 * near + 1] if len(refs) > 2 * near + 1 else None
    _, rows, chunk = mids[0].shape
    groups = rows // coils
    step = pl.program_id(0)
    left = jnp.concatenate([mid[0] for mid in mids], axis=1)
    half = LANES // 2
    lane = lax.broadcasted_iota(jnp.int32, (LANES, chunk), 0)
    odd = (lane >= half) if not second else (lane < half)
    spot = (2 * (lane % half + half * second) + odd.astype(jnp.int32)).astype(jnp.float32)
    told = [note[0].astype(jnp.float32) for note in notes]
    hits = [told[d][ROW_NOTE : ROW_NOTE + 1] + 2.0 * seats[d] == spot for d in range(near)]

    def finish(pair, total):
        low = total[:, :LANES].reshape(groups, 1, coils, LANES)
        high = total[:, LANES:].reshape(groups, 1, coils, LANES)
        both = jnp.concatenate([low, high], axis=1).reshape(groups, 2 * coils, LANES)
        out_ref[:, pair] = both.astype(jnp.bfloat16)

    for pair in range(ranks // 2):
        right = jnp.concatenate(
            [
                jnp.concatenate(
                    [jnp.where(hits[d], told[d][rank : rank + 1], 0.0).astype(jnp.bfloat16) for d in range(near)], axis=1
                )
                for rank in (2 * pair, 2 * pair + 1)
            ],
            axis=0,
        )
        total = dot_nt(left, right)
        if held is None:
            finish(pair, total)
        else:

            @pl.when(step == 0)
            def _(pair=pair, total=total):
                held[pair] = total

            @pl.when(step > 0)
            def _(pair=pair, total=total):
                held[pair] += total

            @pl.when(step == pl.num_programs(0) - 1)
            def _(pair=pair):
                finish(pair, held[pair])


def expand_rows(mids, notes, picks, seats, second, ranks, coils):
    _, rows, depth = mids[0].shape
    near = len(mids)
    chunk = min(depth, CHUNK)
    per = depth // chunk
    groups = rows // coils
    shape = (groups, ranks // 2, 2 * coils, LANES)
    return pl.pallas_call(
        functools.partial(rows_kernel, seats, second, ranks, coils),
        grid=(per,),
        in_specs=[
            *(pl.BlockSpec((1, rows, chunk), lambda k, e=e: (e, 0, k)) for e in picks),
            *(pl.BlockSpec((1, NOTES, chunk), lambda k, e=e: (e, 0, k)) for e in picks),
        ],
        out_specs=pl.BlockSpec(shape, lambda k: (0, 0, 0, 0)),
        out_shape=jax.ShapeDtypeStruct(shape, jnp.bfloat16),
        scratch_shapes=[pltpu.VMEM((ranks // 2, rows, 2 * LANES), jnp.float32)] if per > 1 else [],
        compiler_params=pltpu.CompilerParams(vmem_limit_bytes=28 << 20),
        cost_estimate=pl.CostEstimate(
            flops=2 * rows * near * depth * ranks * LANES, bytes_accessed=2 * rows * ranks * LANES, transcendentals=0
        ),
        name="expand_rows",
    )(*mids, *notes)


def image_kernel(*refs):
    waves_ref, out_ref = refs[-2:]
    plane = out_ref.shape[0]
    half = plane // 2
    firsts = [ref[...] for ref in refs[:-2:2]]
    seconds = [ref[...] for ref in refs[1:-2:2]]
    groups, pairs, inner, _ = firsts[0].shape
    columns = groups * pairs * inner
    lower = lax.broadcasted_iota(jnp.int32, firsts[0].shape, 3) < LANES // 2
    sums = []
    for parity in range(2):
        chosen = zip(firsts, seconds) if parity == 0 else zip(seconds, firsts)
        block = jnp.concatenate([jnp.where(lower, a, b) for a, b in chosen], axis=-1)
        lanes = block.shape[-1]
        block = block.reshape(groups // 2, 2, pairs * inner, lanes)
        crossed = jnp.concatenate([-block[:, 1:2], block[:, 0:1]], axis=1)
        right = jnp.concatenate([block.reshape(columns, lanes), crossed.reshape(columns, lanes)], axis=1)
        sums.append(dot_nt(waves_ref[parity], right))
    out_ref[:half, :] = ((sums[0] + sums[1]) * (1.0 / plane)).astype(jnp.bfloat16)
    out_ref[half:, :] = ((sums[0] - sums[1]) * (1.0 / plane)).astype(jnp.bfloat16)


def form_image(blocks, waves):
    plane = 2 * waves.shape[1]
    groups, pairs, inner, _ = blocks[0].shape
    step = 8
    columns = step * pairs * inner
    return pl.pallas_call(
        image_kernel,
        grid=(groups // step,),
        in_specs=[
            *(pl.BlockSpec((step, pairs, inner, LANES), lambda s: (s, 0, 0, 0)) for _ in blocks),
            pl.BlockSpec(waves.shape, lambda s: (0, 0, 0)),
        ],
        out_specs=pl.BlockSpec((plane, columns), lambda s: (0, s)),
        out_shape=jax.ShapeDtypeStruct((plane, groups * pairs * inner), jnp.bfloat16),
        compiler_params=pltpu.CompilerParams(vmem_limit_bytes=24 << 20),
        cost_estimate=pl.CostEstimate(
            flops=2 * plane * waves.shape[2] * groups * pairs * inner,
            bytes_accessed=4 * plane * groups * pairs * inner,
            transcendentals=0,
        ),
        name="form_image",
    )(*blocks, waves)


def pack_tiles(tiles, tile_rows):
    span = (tile_rows + WIN_ROWS) // 2
    room = LANES // span
    twos = []
    for first in range(0, tiles, room):
        members = list(range(first, min(first + room, tiles)))
        stride = LANES // 2 if len(members) <= 2 and span <= LANES // 2 else span
        twos.append([(t, n * stride) for n, t in enumerate(members)])
    return twos, span


def kx_of_lanes(twos, span, tile_rows):
    at = np.full((2, len(twos) * LANES), -1, np.int32)
    for n, members in enumerate(twos):
        for t, seat in members:
            for k in range(span):
                even = seat + k
                odd = (seat + k + LANES // 2) % LANES
                at[0, n * LANES + even] = (t * tile_rows - 2 + 2 * k) % PLANE
                at[1, n * LANES + odd] = (t * tile_rows - 1 + 2 * k) % PLANE
    return at


def from_tiles(value, source_of):
    count = lax.axis_size("tile")
    return lax.ppermute(value, "tile", [(source_of(t), t) for t in range(count)])


def body(coil_data, frame_of, basis, sample_pos, window_at, live_count):
    parts = coil_data.shape[2]
    tiles = coil_data.shape[3]
    slots = coil_data.shape[4]
    pair = coil_data.shape[5]
    samples = coil_data.shape[6]
    coils = pair // 2
    ranks = basis.shape[1]
    tile_rows = PLANE // tiles
    devices = parts * tiles
    count = devices * slots
    depth = count * WIN_ROWS
    ys = PLANE // tiles
    my_tile = lax.axis_index("tile")
    odd = my_tile % 2

    rates = jnp.broadcast_to(basis[frame_of.reshape(devices, slots)][:, :, None, :], (devices, slots, WIN_ROWS, ranks))
    rates = jnp.pad(rates.reshape(devices, slots * WIN_ROWS, ranks), ((0, 0), (0, 0), (0, samples - ranks)))
    packed = jnp.concatenate([coil_data.reshape(devices, slots * pair, samples), rates], axis=1)
    raw = lax.all_to_all(packed, ("kz", "tile"), split_axis=0, concat_axis=0, tiled=True)

    counts = live_count.reshape(devices)
    slot_idx = jnp.arange(slots, dtype=jnp.int32)
    alive = (slot_idx[None, :] < counts[:, None]).reshape(count, 1, 1)
    pos = jnp.where(alive, sample_pos.reshape(count, 2, samples), FAR_OFF)
    row_k = taper(jnp.arange(WIN_ROWS, dtype=jnp.float32)[None, :, None] - pos[:, 0:1, :])
    col_k = taper(jnp.arange(WIN_COLS, dtype=jnp.float32)[None, :, None] - pos[:, 1:2, :])
    weights = row_k[:, :, None, :] * col_k[:, None, :, :]
    weights = weights.reshape(count, WIN_ROWS * WIN_COLS, samples).astype(jnp.bfloat16)
    corners = window_at.reshape(count, 2)
    win_row = jnp.arange(WIN_ROWS, dtype=jnp.int32)
    from_row = (2 + corners[None, :, 0] + win_row[:, None]).reshape(1, depth)
    col0 = jnp.tile(corners[:, 1], WIN_ROWS).reshape(1, depth)
    place = jnp.concatenate([from_row, col0 // COL_STEP, col0 % COL_STEP], axis=0).astype(jnp.float32)
    place = jnp.pad(place, ((ROW_NOTE, NOTES - ROW_NOTE - 3), (0, 0)))

    cos_tab, sin_tab = wave_tables()
    wave = jnp.asarray(np.concatenate([cos_tab, sin_tab], axis=1))
    wave_rows = lax.dynamic_slice_in_dim(wave, my_tile * ys, ys, 0)
    twos, span = pack_tiles(tiles, tile_rows)
    lane_rows = jnp.asarray(kx_of_lanes(twos, span, tile_rows))
    lane_rows = jnp.where(lane_rows < 0, -1, (lane_rows + (my_tile // 2) * (2 * tile_rows)) % PLANE)
    table, waves = make_tables(wave, wave_rows, lane_rows, coils)

    raw, weights, place, table, waves = lax.optimization_barrier((raw, weights, place, table, waves))
    windows = grid_windows(raw, weights, place, slots, pair)

    pairs = tiles // 2
    mine = [windows]
    for shift in range(1, pairs):
        mine.append(from_tiles(windows, lambda t, shift=shift: (t // 2 + shift) % pairs * 2 + t % 2))
    other = [from_tiles(block, lambda t: t // 2 * 2 + 1 - t % 2) for block in mine]
    odd_ref = odd.astype(jnp.int32).reshape(1)
    mids, notes = zip(
        *(transform_columns(odd_ref, a, b, table, wave_rows, depth, coils) for a, b in zip(mine, other))
    )

    blocks = []
    for members in twos:
        for second in range(2):
            low, high = second * (LANES // 2), (second + 1) * (LANES // 2)
            met = [(t, seat) for t, seat in members if seat < high and seat + span > low]
            blocks.append(
                expand_rows(
                    [mids[t // 2] for t, _ in met],
                    [notes[t // 2] for t, _ in met],
                    [t % 2 for t, _ in met],
                    [float(seat) for _, seat in met],
                    second,
                    ranks,
                    coils,
                )
            )
    return form_image(blocks, waves)[None]


def solution(mesh):
    return jax.shard_map(
        body,
        mesh=mesh,
        in_specs=(
            P("kz", "tile", None, None, None, None, None),
            P("kz", "tile", None, None, None),
            P(),
            P("kz", "tile", None, None, None, None, None),
            P("kz", "tile", None, None, None, None),
            P("kz", "tile", None, None),
        ),
        out_specs=P("kz", None, "tile"),
        check_vma=False,
    )
```

```python
import functools
import math

import jax
import jax.numpy as jnp
import numpy as np
from jax import lax
from jax.experimental import pallas as pl
from jax.experimental.pallas import tpu as pltpu
from jax.sharding import PartitionSpec as P


PLANE = 640
WIN_ROWS = 4
WIN_COLS = 32
LANES = 128
NOTES = 16
ROW_NOTE = 13
COL_HIGH = 14
COL_LOW = 15
COL_STEP = 32
FAR_OFF = -1000.0
CHUNK = 256
NT_DIMS = (((1,), (1,)), ((), ()))


def taper(dist):
    inner = 1.0 - (dist / 1.5) ** 2
    return jnp.maximum(inner, 0.0) ** 2


def wave_tables():
    idx = np.arange(PLANE)
    phase = (idx[:, None] * idx[None, :] % PLANE) * (2.0 * math.pi / PLANE)
    return np.cos(phase).astype(jnp.bfloat16), np.sin(phase).astype(jnp.bfloat16)


def dot_nt(left, right):
    return lax.dot_general(left, right, NT_DIMS, preferred_element_type=jnp.float32)


def unit(shape, dtype=jnp.bfloat16):
    return (lax.broadcasted_iota(jnp.int32, shape, 0) == lax.broadcasted_iota(jnp.int32, shape, 1)).astype(jnp.float32).astype(dtype)


def table_kernel(coils, wave_ref, rows_ref, lanes_ref, out_ref, waves_ref):
    ys = rows_ref.shape[0]
    plane = wave_ref.shape[0]
    rows, width = out_ref.shape
    spot = lax.broadcasted_iota(jnp.int32, (LANES, width), 0)
    lane = lax.broadcasted_iota(jnp.int32, (LANES, width), 1)
    pick = (spot == lane % WIN_COLS).astype(jnp.float32).astype(jnp.bfloat16)
    cos_y = jnp.dot(rows_ref[:, :LANES], pick, preferred_element_type=jnp.float32)
    sin_y = jnp.dot(rows_ref[:, plane : plane + LANES], pick, preferred_element_type=jnp.float32)
    lane = lax.broadcasted_iota(jnp.int32, (ys, width), 1) // WIN_COLS
    into_re = jnp.where(lane < coils, cos_y, -sin_y)
    into_im = jnp.where(lane < coils, sin_y, cos_y)
    both = jnp.concatenate([into_re[:, None, None, :], into_im[:, None, None, :]], axis=1)
    both = jnp.broadcast_to(both, (ys, 2, coils, width))
    mine = lax.broadcasted_iota(jnp.int32, both.shape, 2)
    other = lax.broadcasted_iota(jnp.int32, both.shape, 3) // WIN_COLS % coils
    out_ref[...] = jnp.where(mine == other, both, 0.0).reshape(rows, width).astype(jnp.bfloat16)

    half, double = waves_ref.shape[1:]
    held = double // 2
    row = lax.broadcasted_iota(jnp.int32, (plane, held), 0)
    for parity in range(2):
        pick = (row == lanes_ref[parity : parity + 1, :]).astype(jnp.float32).astype(jnp.bfloat16)
        for part in range(2):
            waves_ref[parity, :, part * held : (part + 1) * held] = jnp.dot(
                wave_ref[:half, part * plane : (part + 1) * plane], pick, preferred_element_type=jnp.float32
            ).astype(jnp.bfloat16)


def make_tables(wave, wave_rows, lane_rows, coils):
    ys = wave_rows.shape[0]
    plane = wave.shape[0]
    return pl.pallas_call(
        functools.partial(table_kernel, coils),
        out_shape=[
            jax.ShapeDtypeStruct((ys * 2 * coils, WIN_COLS * 2 * coils), jnp.bfloat16),
            jax.ShapeDtypeStruct((2, plane // 2, 2 * lane_rows.shape[1]), jnp.bfloat16),
        ],
        compiler_params=pltpu.CompilerParams(vmem_limit_bytes=40 << 20),
        name="make_tables",
    )(wave, wave_rows, lane_rows)


def pack_kernel(frame_ref, data_ref, basis_ref, out_ref, rows_ref, rates_ref):
    parts, tiles, slots, pair, samples = data_ref.shape[2:]
    devices = parts * tiles
    rows_ref[...] = lax.dot_general(
        basis_ref[...], unit((basis_ref.shape[0], samples)), (((0,), (0,)), ((), ())), preferred_element_type=jnp.float32
    )
    out_ref[:, : slots * pair, :] = data_ref[...].reshape(devices, slots * pair, samples)
    rates_ref[...] = jnp.zeros_like(rates_ref)

    @pl.loop(0, parts)
    def _(part):
        for tile in range(tiles):
            for slot in range(slots):
                frame = frame_ref[0, 0, part, slot, tile]
                row = (part * tiles + tile) * (slots * WIN_ROWS) + slot * WIN_ROWS
                rates_ref[pl.ds(row, 1), :] = rows_ref[pl.ds(frame, 1), :]

    out_ref[:, slots * pair :, :] = rates_ref[...].reshape(devices, slots * WIN_ROWS, samples).astype(jnp.bfloat16)


def pack_slots(coil_data, frame_of, basis):
    parts, tiles, slots, pair, samples = coil_data.shape[2:]
    devices = parts * tiles
    return pl.pallas_call(
        pack_kernel,
        in_specs=[
            pl.BlockSpec(memory_space=pltpu.SMEM),
            pl.BlockSpec(memory_space=pltpu.VMEM),
            pl.BlockSpec(memory_space=pltpu.VMEM),
        ],
        out_shape=jax.ShapeDtypeStruct((devices, slots * (pair + WIN_ROWS), samples), jnp.bfloat16),
        scratch_shapes=[
            pltpu.VMEM((basis.shape[0], samples), jnp.float32),
            pltpu.VMEM((devices * slots * WIN_ROWS, samples), jnp.float32),
        ],
        compiler_params=pltpu.CompilerParams(vmem_limit_bytes=60 << 20),
        name="pack_slots",
    )(jnp.swapaxes(frame_of, 3, 4), coil_data, basis.T)


def window_kernel(slots, pair, data_ref, rate_ref, weight_ref, place_ref, out_ref, held, rates):
    sources = data_ref.shape[0]
    count = held.shape[0] // pair
    step = pl.program_id(0)
    for q in range(sources * slots):
        data = data_ref[q // slots, (q % slots) * pair : (q % slots + 1) * pair]
        first = (step * sources * slots + q) * pair
        held[pl.ds(pl.multiple_of(first, pair), pair), :] = dot_nt(data, weight_ref[q])

    @pl.when(step == pl.num_programs(0) - 1)
    def _():
        depth = place_ref.shape[1]
        width = out_ref.shape[1]
        per = LANES // WIN_COLS
        lane = lax.broadcasted_iota(jnp.int32, (count, LANES), 1) // WIN_COLS
        for group in range(pair // per):
            rows = [held[pl.ds(group * per + q, count, stride=pair), :] for q in range(per)]
            for i in range(WIN_ROWS):
                total = None
                for q in range(per):
                    turn = (q - i) % per * WIN_COLS
                    moved = pltpu.roll(rows[q], turn, 1) if turn else rows[q]
                    total = moved if total is None else jnp.where(lane == q, moved, total)
                out_ref[i * count : (i + 1) * count, group * LANES : (group + 1) * LANES] = total.astype(jnp.bfloat16)
        rates[...] = rate_ref[...].astype(jnp.float32).reshape(rates.shape)
        once = rates[pl.ds(0, count, stride=WIN_ROWS), :].astype(jnp.bfloat16)
        notes = dot_nt(unit((NOTES, LANES)), jnp.concatenate([once] * WIN_ROWS, axis=0)) + place_ref[...]
        lanes = min(depth, width)
        for part in range(depth // lanes):
            part_rows = notes[:, part * lanes : (part + 1) * lanes]
            if lanes < width:
                part_rows = jnp.concatenate([part_rows, jnp.zeros((NOTES, width - lanes), jnp.float32)], axis=1)
            out_ref[depth + part * NOTES : depth + (part + 1) * NOTES, :] = part_rows.astype(jnp.bfloat16)


def grid_windows(raw, weights, place, slots, pair):
    devices, _, samples = raw.shape
    count = devices * slots
    depth = count * WIN_ROWS
    width = WIN_COLS * pair
    sources = 8
    rate_rows = slots * WIN_ROWS
    total_rows = depth + NOTES * (depth // min(depth, width))
    return pl.pallas_call(
        functools.partial(window_kernel, slots, pair),
        grid=(devices // sources,),
        in_specs=[
            pl.BlockSpec((sources, slots * pair, samples), lambda s: (s, 0, 0)),
            pl.BlockSpec((devices, rate_rows, samples), lambda s: (0, slots * pair // rate_rows, 0)),
            pl.BlockSpec((sources * slots, LANES, samples), lambda s: (s, 0, 0)),
            pl.BlockSpec((NOTES, depth), lambda s: (0, 0)),
        ],
        out_specs=pl.BlockSpec((total_rows, width), lambda s: (0, 0)),
        out_shape=jax.ShapeDtypeStruct((total_rows, width), jnp.bfloat16),
        scratch_shapes=[
            pltpu.VMEM((count * pair, LANES), jnp.float32),
            pltpu.VMEM((devices * rate_rows, LANES), jnp.float32),
        ],
        compiler_params=pltpu.CompilerParams(vmem_limit_bytes=24 << 20),
        name="grid_windows",
    )(raw, raw, weights, place)


def columns_kernel(coils, odd_ref, mine_ref, mine_notes, other_ref, other_notes, table_ref, wave_ref, out_ref, notes_ref):
    rows = table_ref.shape[0]
    ys = rows // (2 * coils)
    plane = wave_ref.shape[1] // 2
    depth = mine_ref.shape[0]
    take_mine = odd_ref[0] == pl.program_id(0)
    grids = jnp.where(take_mine, mine_ref[...], other_ref[...])
    notes = jnp.where(take_mine, mine_notes[...], other_notes[...])
    notes_ref[0] = notes
    notes = notes.astype(jnp.float32)
    col0 = notes[COL_HIGH : COL_HIGH + 1] * COL_STEP + notes[COL_LOW : COL_LOW + 1]
    row = lax.broadcasted_iota(jnp.int32, (plane, depth), 0).astype(jnp.float32)
    corner = (row == col0).astype(jnp.float32).astype(jnp.bfloat16)
    turn_re = jnp.dot(wave_ref[:, :plane], corner, preferred_element_type=jnp.float32)[:, None, :]
    turn_im = jnp.dot(wave_ref[:, plane:], corner, preferred_element_type=jnp.float32)[:, None, :]
    flat = dot_nt(table_ref[...], grids).reshape(ys, 2, coils, depth)
    real, imag = flat[:, 0], flat[:, 1]
    done_re = real * turn_re - imag * turn_im
    done_im = real * turn_im + imag * turn_re
    both = jnp.concatenate([done_re[:, None], done_im[:, None]], axis=1)
    out_ref[0] = both.reshape(rows, depth).astype(jnp.bfloat16)


def transform_columns(odd, mine, other, table, wave_rows, depth, coils):
    width = mine.shape[1]
    rows = table.shape[0]
    ys, waves = wave_rows.shape
    chunk = min(depth, CHUNK)
    per = depth // chunk
    grid_spec = pl.BlockSpec((chunk, width), lambda e, k: (k, 0))
    note_spec = pl.BlockSpec(
        (NOTES, chunk), lambda e, k: (depth // NOTES + k * chunk // width, k * chunk % width // chunk)
    )
    return pl.pallas_call(
        functools.partial(columns_kernel, coils),
        grid=(2, per),
        in_specs=[
            pl.BlockSpec(memory_space=pltpu.SMEM),
            grid_spec,
            note_spec,
            grid_spec,
            note_spec,
            pl.BlockSpec((rows, width), lambda e, k: (0, 0)),
            pl.BlockSpec((ys, waves), lambda e, k: (0, 0)),
        ],
        out_specs=[
            pl.BlockSpec((1, rows, chunk), lambda e, k: (e, 0, k)),
            pl.BlockSpec((1, NOTES, chunk), lambda e, k: (e, 0, k)),
        ],
        out_shape=[
            jax.ShapeDtypeStruct((2, rows, depth), jnp.bfloat16),
            jax.ShapeDtypeStruct((2, NOTES, depth), jnp.bfloat16),
        ],
        compiler_params=pltpu.CompilerParams(vmem_limit_bytes=28 << 20),
        cost_estimate=pl.CostEstimate(
            flops=2 * 2 * rows * width * depth, bytes_accessed=2 * 2 * rows * depth, transcendentals=0
        ),
        name="transform_columns",
    )(odd, mine, mine, other, other, table, wave_rows)


def rows_kernel(seats, second, ranks, coils, *refs):
    near = len(seats)
    mids = refs[:near]
    notes = refs[near : 2 * near]
    out_ref = refs[2 * near]
    held = refs[2 * near + 1] if len(refs) > 2 * near + 1 else None
    _, rows, chunk = mids[0].shape
    groups = rows // coils
    step = pl.program_id(0)
    left = jnp.concatenate([mid[0] for mid in mids], axis=1)
    half = LANES // 2
    lane = lax.broadcasted_iota(jnp.int32, (LANES, chunk), 0)
    odd = (lane >= half) if not second else (lane < half)
    spot = (2 * (lane % half + half * second) + odd.astype(jnp.int32)).astype(jnp.float32)
    told = [note[0].astype(jnp.float32) for note in notes]
    hits = [told[d][ROW_NOTE : ROW_NOTE + 1] + 2.0 * seats[d] == spot for d in range(near)]

    def finish(pair, total):
        low = total[:, :LANES].reshape(groups, 1, coils, LANES)
        high = total[:, LANES:].reshape(groups, 1, coils, LANES)
        both = jnp.concatenate([low, high], axis=1).reshape(groups, 2 * coils, LANES)
        out_ref[:, pair] = both.astype(jnp.bfloat16)

    for pair in range(ranks // 2):
        right = jnp.concatenate(
            [
                jnp.concatenate(
                    [jnp.where(hits[d], told[d][rank : rank + 1], 0.0).astype(jnp.bfloat16) for d in range(near)], axis=1
                )
                for rank in (2 * pair, 2 * pair + 1)
            ],
            axis=0,
        )
        total = dot_nt(left, right)
        if held is None:
            finish(pair, total)
        else:

            @pl.when(step == 0)
            def _(pair=pair, total=total):
                held[pair] = total

            @pl.when(step > 0)
            def _(pair=pair, total=total):
                held[pair] += total

            @pl.when(step == pl.num_programs(0) - 1)
            def _(pair=pair):
                finish(pair, held[pair])


def expand_rows(mids, notes, picks, seats, second, ranks, coils):
    _, rows, depth = mids[0].shape
    near = len(mids)
    chunk = min(depth, CHUNK)
    per = depth // chunk
    groups = rows // coils
    shape = (groups, ranks // 2, 2 * coils, LANES)
    return pl.pallas_call(
        functools.partial(rows_kernel, seats, second, ranks, coils),
        grid=(per,),
        in_specs=[
            *(pl.BlockSpec((1, rows, chunk), lambda k, e=e: (e, 0, k)) for e in picks),
            *(pl.BlockSpec((1, NOTES, chunk), lambda k, e=e: (e, 0, k)) for e in picks),
        ],
        out_specs=pl.BlockSpec(shape, lambda k: (0, 0, 0, 0)),
        out_shape=jax.ShapeDtypeStruct(shape, jnp.bfloat16),
        scratch_shapes=[pltpu.VMEM((ranks // 2, rows, 2 * LANES), jnp.float32)] if per > 1 else [],
        compiler_params=pltpu.CompilerParams(vmem_limit_bytes=28 << 20),
        cost_estimate=pl.CostEstimate(
            flops=2 * rows * near * depth * ranks * LANES, bytes_accessed=2 * rows * ranks * LANES, transcendentals=0
        ),
        name="expand_rows",
    )(*mids, *notes)


def image_kernel(*refs):
    waves_ref, out_ref = refs[-2:]
    plane = out_ref.shape[0]
    half = plane // 2
    firsts = [ref[...] for ref in refs[:-2:2]]
    seconds = [ref[...] for ref in refs[1:-2:2]]
    groups, pairs, inner, _ = firsts[0].shape
    columns = groups * pairs * inner
    lower = lax.broadcasted_iota(jnp.int32, firsts[0].shape, 3) < LANES // 2
    sums = []
    for parity in range(2):
        chosen = zip(firsts, seconds) if parity == 0 else zip(seconds, firsts)
        block = jnp.concatenate([jnp.where(lower, a, b) for a, b in chosen], axis=-1)
        lanes = block.shape[-1]
        block = block.reshape(groups // 2, 2, pairs * inner, lanes)
        crossed = jnp.concatenate([-block[:, 1:2], block[:, 0:1]], axis=1)
        right = jnp.concatenate([block.reshape(columns, lanes), crossed.reshape(columns, lanes)], axis=1)
        sums.append(dot_nt(waves_ref[parity], right))
    out_ref[:half, :] = ((sums[0] + sums[1]) * (1.0 / plane)).astype(jnp.bfloat16)
    out_ref[half:, :] = ((sums[0] - sums[1]) * (1.0 / plane)).astype(jnp.bfloat16)


def form_image(blocks, waves):
    plane = 2 * waves.shape[1]
    groups, pairs, inner, _ = blocks[0].shape
    step = next(n for n in (16, 8, 4, 2) if groups % n == 0)
    columns = step * pairs * inner
    return pl.pallas_call(
        image_kernel,
        grid=(groups // step,),
        in_specs=[
            *(pl.BlockSpec((step, pairs, inner, LANES), lambda s: (s, 0, 0, 0)) for _ in blocks),
            pl.BlockSpec(waves.shape, lambda s: (0, 0, 0)),
        ],
        out_specs=pl.BlockSpec((plane, columns), lambda s: (0, s)),
        out_shape=jax.ShapeDtypeStruct((plane, groups * pairs * inner), jnp.bfloat16),
        compiler_params=pltpu.CompilerParams(vmem_limit_bytes=24 << 20),
        cost_estimate=pl.CostEstimate(
            flops=2 * plane * waves.shape[2] * groups * pairs * inner,
            bytes_accessed=4 * plane * groups * pairs * inner,
            transcendentals=0,
        ),
        name="form_image",
    )(*blocks, waves)


def pack_tiles(tiles, tile_rows):
    span = (tile_rows + WIN_ROWS) // 2
    room = LANES // span
    twos = []
    for first in range(0, tiles, room):
        members = list(range(first, min(first + room, tiles)))
        stride = LANES // 2 if len(members) <= 2 and span <= LANES // 2 else span
        twos.append([(t, n * stride) for n, t in enumerate(members)])
    return twos, span


def kx_of_lanes(twos, span):
    at = np.full((2, 2, len(twos) * LANES), -1, np.int32)
    for n, members in enumerate(twos):
        for t, seat in members:
            for k in range(span):
                even = seat + k
                odd = (seat + k + LANES // 2) % LANES
                at[:, 0, n * LANES + even] = t, 2 * k
                at[:, 1, n * LANES + odd] = t, 2 * k + 1
    return at


def from_tiles(value, source_of):
    count = lax.axis_size("tile")
    return lax.ppermute(value, "tile", [(source_of(t), t) for t in range(count)])


def body(coil_data, frame_of, basis, sample_pos, window_at, live_count):
    parts = coil_data.shape[2]
    tiles = coil_data.shape[3]
    slots = coil_data.shape[4]
    pair = coil_data.shape[5]
    samples = coil_data.shape[6]
    coils = pair // 2
    ranks = basis.shape[1]
    tile_rows = PLANE // tiles
    devices = parts * tiles
    count = devices * slots
    depth = count * WIN_ROWS
    ys = PLANE // tiles
    my_tile = lax.axis_index("tile")
    odd = my_tile % 2

    packed = pack_slots(coil_data, frame_of, basis)
    raw = lax.all_to_all(packed, ("kz", "tile"), split_axis=0, concat_axis=0, tiled=True)

    counts = live_count.reshape(devices)
    slot_idx = jnp.arange(slots, dtype=jnp.int32)
    alive = (slot_idx[None, :] < counts[:, None]).reshape(count, 1, 1)
    pos = jnp.where(alive, sample_pos.reshape(count, 2, samples), FAR_OFF)
    row_k = taper(jnp.arange(WIN_ROWS, dtype=jnp.float32)[None, :, None] - pos[:, 0:1, :])
    col_k = taper(jnp.arange(WIN_COLS, dtype=jnp.float32)[None, :, None] - pos[:, 1:2, :])
    weights = row_k[:, :, None, :] * col_k[:, None, :, :]
    weights = weights.reshape(count, WIN_ROWS * WIN_COLS, samples).astype(jnp.bfloat16)
    corners = window_at.reshape(count, 2)
    win_row = jnp.arange(WIN_ROWS, dtype=jnp.int32)
    from_row = (2 + corners[None, :, 0] + win_row[:, None]).reshape(1, depth)
    col0 = jnp.tile(corners[:, 1], WIN_ROWS).reshape(1, depth)
    place = jnp.concatenate([from_row, col0 // COL_STEP, col0 % COL_STEP], axis=0).astype(jnp.float32)
    place = jnp.pad(place, ((ROW_NOTE, NOTES - ROW_NOTE - 3), (0, 0)))

    cos_tab, sin_tab = wave_tables()
    wave = jnp.asarray(np.concatenate([cos_tab, sin_tab], axis=1))
    wave_rows = lax.dynamic_slice_in_dim(wave, my_tile * ys, ys, 0)
    twos, span = pack_tiles(tiles, tile_rows)
    arrival, window_row = (jnp.asarray(part) for part in kx_of_lanes(twos, span))
    lane_tile = (arrival // 2 ^ my_tile // 2) * 2 + arrival % 2
    lane_rows = jnp.where(arrival < 0, -1, (lane_tile * tile_rows - 2 + window_row + PLANE) % PLANE)
    table, waves = make_tables(wave, wave_rows, lane_rows, coils)

    raw, weights, place, table, waves = lax.optimization_barrier((raw, weights, place, table, waves))
    windows = grid_windows(raw, weights, place, slots, pair)

    pairs = tiles // 2
    mine, other = [windows], []
    for hop in range(1, pairs):
        near = hop & -hop
        mine.append(from_tiles(mine[hop - near], lambda t, near=near: (t // 2 ^ near) * 2 + t % 2))
    for hop in range(pairs):
        other.append(from_tiles(mine[hop], lambda t: t // 2 * 2 + 1 - t % 2))
    odd_ref = odd.astype(jnp.int32).reshape(1)
    mids, notes = [], []
    for hop in range(pairs):
        mid, note = transform_columns(odd_ref, mine[hop], other[hop], table, wave_rows, depth, coils)
        mids.append(mid)
        notes.append(note)

    blocks = []
    for members in twos:
        for second in range(2):
            low, high = second * (LANES // 2), (second + 1) * (LANES // 2)
            met = [(t, seat) for t, seat in members if seat < high and seat + span > low]
            block = expand_rows(
                [mids[t // 2] for t, _ in met],
                [notes[t // 2] for t, _ in met],
                [t % 2 for t, _ in met],
                [float(seat) for _, seat in met],
                second,
                ranks,
                coils,
            )
            blocks.append(block)
    return form_image(blocks, waves)[None]


def solution(mesh):
    return jax.shard_map(
        body,
        mesh=mesh,
        in_specs=(
            P("kz", "tile", None, None, None, None, None),
            P("kz", "tile", None, None, None),
            P(),
            P("kz", "tile", None, None, None, None, None),
            P("kz", "tile", None, None, None, None),
            P("kz", "tile", None, None),
        ),
        out_specs=P("kz", None, "tile"),
        check_vma=False,
    )
```

```python
import functools
import math

import jax
import jax.numpy as jnp
import numpy as np
from jax import lax
from jax.experimental import pallas as pl
from jax.experimental.pallas import tpu as pltpu
from jax.sharding import PartitionSpec as P


PLANE = 640
WIN_ROWS = 4
WIN_COLS = 32
LANES = 128
NOTES = 16
ROW_NOTE = 13
COL_HIGH = 14
COL_LOW = 15
COL_STEP = 32
FAR_OFF = -1000.0
CHUNK = 256
NT_DIMS = (((1,), (1,)), ((), ()))


def taper(dist):
    inner = 1.0 - (dist / 1.5) ** 2
    return jnp.maximum(inner, 0.0) ** 2


def wave_tables():
    idx = np.arange(PLANE)
    phase = (idx[:, None] * idx[None, :] % PLANE) * (2.0 * math.pi / PLANE)
    return np.cos(phase).astype(jnp.bfloat16), np.sin(phase).astype(jnp.bfloat16)


def dot_nt(left, right):
    return lax.dot_general(left, right, NT_DIMS, preferred_element_type=jnp.float32)


def unit(shape, dtype=jnp.bfloat16):
    return (lax.broadcasted_iota(jnp.int32, shape, 0) == lax.broadcasted_iota(jnp.int32, shape, 1)).astype(jnp.float32).astype(dtype)


def table_kernel(coils, wave_ref, rows_ref, lanes_ref, out_ref, waves_ref):
    ys = rows_ref.shape[0]
    plane = wave_ref.shape[0]
    rows, width = out_ref.shape
    spot = lax.broadcasted_iota(jnp.int32, (LANES, width), 0)
    lane = lax.broadcasted_iota(jnp.int32, (LANES, width), 1)
    pick = (spot == lane % WIN_COLS).astype(jnp.float32).astype(jnp.bfloat16)
    cos_y = jnp.dot(rows_ref[:, :LANES], pick, preferred_element_type=jnp.float32)
    sin_y = jnp.dot(rows_ref[:, plane : plane + LANES], pick, preferred_element_type=jnp.float32)
    lane = lax.broadcasted_iota(jnp.int32, (ys, width), 1) // WIN_COLS
    into_re = jnp.where(lane < coils, cos_y, -sin_y)
    into_im = jnp.where(lane < coils, sin_y, cos_y)
    both = jnp.concatenate([into_re[:, None, None, :], into_im[:, None, None, :]], axis=1)
    both = jnp.broadcast_to(both, (ys, 2, coils, width))
    mine = lax.broadcasted_iota(jnp.int32, both.shape, 2)
    other = lax.broadcasted_iota(jnp.int32, both.shape, 3) // WIN_COLS % coils
    out_ref[...] = jnp.where(mine == other, both, 0.0).reshape(rows, width).astype(jnp.bfloat16)

    half, double = waves_ref.shape[1:]
    held = double // 2
    row = lax.broadcasted_iota(jnp.int32, (plane, held), 0)
    for parity in range(2):
        pick = (row == lanes_ref[parity : parity + 1, :]).astype(jnp.float32).astype(jnp.bfloat16)
        for part in range(2):
            waves_ref[parity, :, part * held : (part + 1) * held] = jnp.dot(
                wave_ref[:half, part * plane : (part + 1) * plane], pick, preferred_element_type=jnp.float32
            ).astype(jnp.bfloat16)


def make_tables(wave, wave_rows, lane_rows, coils):
    ys = wave_rows.shape[0]
    plane = wave.shape[0]
    return pl.pallas_call(
        functools.partial(table_kernel, coils),
        out_shape=[
            jax.ShapeDtypeStruct((ys * 2 * coils, WIN_COLS * 2 * coils), jnp.bfloat16),
            jax.ShapeDtypeStruct((2, plane // 2, 2 * lane_rows.shape[1]), jnp.bfloat16),
        ],
        compiler_params=pltpu.CompilerParams(vmem_limit_bytes=40 << 20),
        name="make_tables",
    )(wave, wave_rows, lane_rows)


def pack_kernel(frame_ref, data_ref, basis_ref, out_ref, rows_ref, rates_ref):
    parts, tiles, slots, pair, samples = data_ref.shape[2:]
    devices = parts * tiles
    rows_ref[...] = lax.dot_general(
        basis_ref[...], unit((basis_ref.shape[0], samples)), (((0,), (0,)), ((), ())), preferred_element_type=jnp.float32
    )
    out_ref[:, : slots * pair, :] = data_ref[...].reshape(devices, slots * pair, samples)
    rates_ref[...] = jnp.zeros_like(rates_ref)

    @pl.loop(0, parts)
    def _(part):
        for tile in range(tiles):
            for slot in range(slots):
                frame = frame_ref[0, 0, part, slot, tile]
                row = (part * tiles + tile) * (slots * WIN_ROWS) + slot * WIN_ROWS
                rates_ref[pl.ds(row, 1), :] = rows_ref[pl.ds(frame, 1), :]

    out_ref[:, slots * pair :, :] = rates_ref[...].reshape(devices, slots * WIN_ROWS, samples).astype(jnp.bfloat16)


def pack_slots(coil_data, frame_of, basis):
    parts, tiles, slots, pair, samples = coil_data.shape[2:]
    devices = parts * tiles
    return pl.pallas_call(
        pack_kernel,
        in_specs=[
            pl.BlockSpec(memory_space=pltpu.SMEM),
            pl.BlockSpec(memory_space=pltpu.VMEM),
            pl.BlockSpec(memory_space=pltpu.VMEM),
        ],
        out_shape=jax.ShapeDtypeStruct((devices, slots * (pair + WIN_ROWS), samples), jnp.bfloat16),
        scratch_shapes=[
            pltpu.VMEM((basis.shape[0], samples), jnp.float32),
            pltpu.VMEM((devices * slots * WIN_ROWS, samples), jnp.float32),
        ],
        compiler_params=pltpu.CompilerParams(vmem_limit_bytes=60 << 20),
        name="pack_slots",
    )(jnp.swapaxes(frame_of, 3, 4), coil_data, basis.T)


def window_kernel(slots, pair, data_ref, rate_ref, weight_ref, place_ref, out_ref, held, rates):
    sources = data_ref.shape[0]
    count = held.shape[0] // pair
    step = pl.program_id(0)
    for q in range(sources * slots):
        data = data_ref[q // slots, (q % slots) * pair : (q % slots + 1) * pair]
        first = (step * sources * slots + q) * pair
        held[pl.ds(pl.multiple_of(first, pair), pair), :] = dot_nt(data, weight_ref[q])

    @pl.when(step == pl.num_programs(0) - 1)
    def _():
        depth = place_ref.shape[1]
        width = out_ref.shape[1]
        per = LANES // WIN_COLS
        lane = lax.broadcasted_iota(jnp.int32, (count, LANES), 1) // WIN_COLS
        for group in range(pair // per):
            rows = [held[pl.ds(group * per + q, count, stride=pair), :] for q in range(per)]
            for i in range(WIN_ROWS):
                total = None
                for q in range(per):
                    turn = (q - i) % per * WIN_COLS
                    moved = pltpu.roll(rows[q], turn, 1) if turn else rows[q]
                    total = moved if total is None else jnp.where(lane == q, moved, total)
                out_ref[i * count : (i + 1) * count, group * LANES : (group + 1) * LANES] = total.astype(jnp.bfloat16)
        rates[...] = rate_ref[...].astype(jnp.float32).reshape(rates.shape)
        once = rates[pl.ds(0, count, stride=WIN_ROWS), :].astype(jnp.bfloat16)
        notes = dot_nt(unit((NOTES, LANES)), jnp.concatenate([once] * WIN_ROWS, axis=0)) + place_ref[...]
        lanes = min(depth, width)
        for part in range(depth // lanes):
            part_rows = notes[:, part * lanes : (part + 1) * lanes]
            if lanes < width:
                part_rows = jnp.concatenate([part_rows, jnp.zeros((NOTES, width - lanes), jnp.float32)], axis=1)
            out_ref[depth + part * NOTES : depth + (part + 1) * NOTES, :] = part_rows.astype(jnp.bfloat16)


def grid_windows(raw, weights, place, slots, pair):
    devices, _, samples = raw.shape
    count = devices * slots
    depth = count * WIN_ROWS
    width = WIN_COLS * pair
    sources = 8
    rate_rows = slots * WIN_ROWS
    total_rows = depth + NOTES * (depth // min(depth, width))
    return pl.pallas_call(
        functools.partial(window_kernel, slots, pair),
        grid=(devices // sources,),
        in_specs=[
            pl.BlockSpec((sources, slots * pair, samples), lambda s: (s, 0, 0)),
            pl.BlockSpec((devices, rate_rows, samples), lambda s: (0, slots * pair // rate_rows, 0)),
            pl.BlockSpec((sources * slots, LANES, samples), lambda s: (s, 0, 0)),
            pl.BlockSpec((NOTES, depth), lambda s: (0, 0)),
        ],
        out_specs=pl.BlockSpec((total_rows, width), lambda s: (0, 0)),
        out_shape=jax.ShapeDtypeStruct((total_rows, width), jnp.bfloat16),
        scratch_shapes=[
            pltpu.VMEM((count * pair, LANES), jnp.float32),
            pltpu.VMEM((devices * rate_rows, LANES), jnp.float32),
        ],
        compiler_params=pltpu.CompilerParams(vmem_limit_bytes=24 << 20),
        name="grid_windows",
    )(raw, raw, weights, place)


def columns_kernel(coils, odd_ref, mine_ref, mine_notes, other_ref, other_notes, table_ref, wave_ref, out_ref, notes_ref):
    rows = table_ref.shape[0]
    ys = rows // (2 * coils)
    plane = wave_ref.shape[1] // 2
    depth = mine_ref.shape[0]
    take_mine = odd_ref[0] == pl.program_id(0)
    grids = jnp.where(take_mine, mine_ref[...], other_ref[...])
    notes = jnp.where(take_mine, mine_notes[...], other_notes[...])
    notes_ref[0] = notes
    notes = notes.astype(jnp.float32)
    col0 = notes[COL_HIGH : COL_HIGH + 1] * COL_STEP + notes[COL_LOW : COL_LOW + 1]
    row = lax.broadcasted_iota(jnp.int32, (plane, depth), 0).astype(jnp.float32)
    corner = (row == col0).astype(jnp.float32).astype(jnp.bfloat16)
    turn_re = jnp.dot(wave_ref[:, :plane], corner, preferred_element_type=jnp.float32)[:, None, :]
    turn_im = jnp.dot(wave_ref[:, plane:], corner, preferred_element_type=jnp.float32)[:, None, :]
    flat = dot_nt(table_ref[...], grids).reshape(ys, 2, coils, depth)
    real, imag = flat[:, 0], flat[:, 1]
    done_re = real * turn_re - imag * turn_im
    done_im = real * turn_im + imag * turn_re
    both = jnp.concatenate([done_re[:, None], done_im[:, None]], axis=1)
    out_ref[0] = both.reshape(rows, depth).astype(jnp.bfloat16)


def transform_columns(odd, mine, other, table, wave_rows, depth, coils):
    width = mine.shape[1]
    rows = table.shape[0]
    ys, waves = wave_rows.shape
    chunk = min(depth, CHUNK)
    per = depth // chunk
    grid_spec = pl.BlockSpec((chunk, width), lambda e, k: (k, 0))
    note_spec = pl.BlockSpec(
        (NOTES, chunk), lambda e, k: (depth // NOTES + k * chunk // width, k * chunk % width // chunk)
    )
    return pl.pallas_call(
        functools.partial(columns_kernel, coils),
        grid=(2, per),
        in_specs=[
            pl.BlockSpec(memory_space=pltpu.SMEM),
            grid_spec,
            note_spec,
            grid_spec,
            note_spec,
            pl.BlockSpec((rows, width), lambda e, k: (0, 0)),
            pl.BlockSpec((ys, waves), lambda e, k: (0, 0)),
        ],
        out_specs=[
            pl.BlockSpec((1, rows, chunk), lambda e, k: (e, 0, k)),
            pl.BlockSpec((1, NOTES, chunk), lambda e, k: (e, 0, k)),
        ],
        out_shape=[
            jax.ShapeDtypeStruct((2, rows, depth), jnp.bfloat16),
            jax.ShapeDtypeStruct((2, NOTES, depth), jnp.bfloat16),
        ],
        compiler_params=pltpu.CompilerParams(vmem_limit_bytes=28 << 20),
        cost_estimate=pl.CostEstimate(
            flops=2 * 2 * rows * width * depth, bytes_accessed=2 * 2 * rows * depth, transcendentals=0
        ),
        name="transform_columns",
    )(odd, mine, mine, other, other, table, wave_rows)


def rows_kernel(seats, second, mirror, ranks, coils, *refs):
    near = len(seats)
    mids = refs[:near]
    notes = refs[near : 2 * near]
    out_ref = refs[2 * near]
    held = refs[2 * near + 1] if len(refs) > 2 * near + 1 else None
    _, rows, chunk = mids[0].shape
    groups = rows // coils
    step = pl.program_id(0)
    left = jnp.concatenate([mid[0] for mid in mids], axis=1)
    half = LANES // 2
    lane = lax.broadcasted_iota(jnp.int32, (LANES, chunk), 0)
    odd = (lane >= half) if not second else (lane < half)
    spot = (2 * (lane % half) + odd.astype(jnp.int32)).astype(jnp.float32)
    told = [note[0].astype(jnp.float32) for note in notes]
    rows_told = [note[ROW_NOTE : ROW_NOTE + 1] for note in told]
    if mirror is not None:
        rows_told = [mirror - note for note in rows_told]
    hits = [rows_told[d] + 2.0 * seats[d] == spot for d in range(near)]

    def finish(pair, total):
        low = total[:, :LANES].reshape(groups, 1, coils, LANES)
        high = total[:, LANES:].reshape(groups, 1, coils, LANES)
        both = jnp.concatenate([low, high], axis=1).reshape(groups, 2 * coils, LANES)
        out_ref[:, pair] = both.astype(jnp.bfloat16)

    for pair in range(ranks // 2):
        right = jnp.concatenate(
            [
                jnp.concatenate(
                    [jnp.where(hits[d], told[d][rank : rank + 1], 0.0).astype(jnp.bfloat16) for d in range(near)], axis=1
                )
                for rank in (2 * pair, 2 * pair + 1)
            ],
            axis=0,
        )
        total = dot_nt(left, right)
        if held is None:
            finish(pair, total)
        else:

            @pl.when(step == 0)
            def _(pair=pair, total=total):
                held[pair] = total

            @pl.when(step > 0)
            def _(pair=pair, total=total):
                held[pair] += total

            @pl.when(step == pl.num_programs(0) - 1)
            def _(pair=pair):
                finish(pair, held[pair])


def expand_rows(mids, notes, picks, seats, second, mirror, ranks, coils):
    _, rows, depth = mids[0].shape
    near = len(mids)
    chunk = min(depth, CHUNK)
    per = depth // chunk
    groups = rows // coils
    shape = (groups, ranks // 2, 2 * coils, LANES)
    return pl.pallas_call(
        functools.partial(rows_kernel, seats, second, mirror, ranks, coils),
        grid=(per,),
        in_specs=[
            *(pl.BlockSpec((1, rows, chunk), lambda k, e=e: (e, 0, k)) for e in picks),
            *(pl.BlockSpec((1, NOTES, chunk), lambda k, e=e: (e, 0, k)) for e in picks),
        ],
        out_specs=pl.BlockSpec(shape, lambda k: (0, 0, 0, 0)),
        out_shape=jax.ShapeDtypeStruct(shape, jnp.bfloat16),
        scratch_shapes=[pltpu.VMEM((ranks // 2, rows, 2 * LANES), jnp.float32)] if per > 1 else [],
        compiler_params=pltpu.CompilerParams(vmem_limit_bytes=28 << 20),
        cost_estimate=pl.CostEstimate(
            flops=2 * rows * near * depth * ranks * LANES, bytes_accessed=2 * rows * ranks * LANES, transcendentals=0
        ),
        name="expand_rows",
    )(*mids, *notes)


def image_kernel(count, *refs):
    waves_ref, out_ref = refs[-2:]
    plane = out_ref.shape[0]
    half = plane // 2
    groups, pairs, inner, _ = refs[0].shape
    columns = groups * pairs * inner
    sums, turns = [], []
    for direct, mirrored in zip(refs[:count], refs[count : 2 * count]):
        ahead, behind = direct[...], mirrored[...]
        sums.append(ahead + behind)
        gap = (ahead - behind).reshape(groups // 2, 2, pairs, inner, LANES)
        turns.append(jnp.concatenate([-gap[:, 1:2], gap[:, 0:1]], axis=1).reshape(ahead.shape))
    lower = lax.broadcasted_iota(jnp.int32, refs[0].shape, 3) < LANES // 2
    halves = []
    for parity in range(2):
        chosen = [
            jnp.where(lower, part[n + parity], part[n + 1 - parity]).reshape(columns, LANES)
            for part in (sums, turns)
            for n in range(0, count, 2)
        ]
        halves.append(dot_nt(waves_ref[parity], jnp.concatenate(chosen, axis=1)))
    out_ref[:half, :] = ((halves[0] + halves[1]) * (1.0 / plane)).astype(jnp.bfloat16)
    out_ref[half:, :] = ((halves[0] - halves[1]) * (1.0 / plane)).astype(jnp.bfloat16)


def form_image(direct, mirrored, waves):
    plane = 2 * waves.shape[1]
    groups, pairs, inner, _ = direct[0].shape
    step = next(n for n in (16, 8, 4, 2) if groups % n == 0)
    columns = step * pairs * inner
    return pl.pallas_call(
        functools.partial(image_kernel, len(direct)),
        grid=(groups // step,),
        in_specs=[
            *(pl.BlockSpec((step, pairs, inner, LANES), lambda s: (s, 0, 0, 0)) for _ in (*direct, *mirrored)),
            pl.BlockSpec(waves.shape, lambda s: (0, 0, 0)),
        ],
        out_specs=pl.BlockSpec((plane, columns), lambda s: (0, s)),
        out_shape=jax.ShapeDtypeStruct((plane, groups * pairs * inner), jnp.bfloat16),
        compiler_params=pltpu.CompilerParams(vmem_limit_bytes=24 << 20),
        cost_estimate=pl.CostEstimate(
            flops=2 * plane * waves.shape[2] * groups * pairs * inner,
            bytes_accessed=4 * plane * groups * pairs * inner,
            transcendentals=0,
        ),
        name="form_image",
    )(*direct, *mirrored, waves)


def pack_tiles(tiles, tile_rows):
    span = (tile_rows + WIN_ROWS) // 2 + 1
    room = LANES // 2 // span
    blocks = []
    for first in range(0, tiles // 2, room):
        blocks.append([(t, n * span) for n, t in enumerate(range(first, min(first + room, tiles // 2)))])
    return blocks + [[]] * (len(blocks) % 2), span


def kx_of_lanes(blocks, span):
    half = LANES // 2
    at = np.full((2, 2, len(blocks) * half), -1, np.int32)
    for n, members in enumerate(blocks):
        for t, seat in members:
            for k in range(span):
                lane = n // 2 * LANES + seat + k
                at[:, 0, lane + half * (n % 2)] = t, 2 * k
                at[:, 1, lane + half * (1 - n % 2)] = t, 2 * k + 1
    return at


def from_tiles(value, source_of):
    count = lax.axis_size("tile")
    return lax.ppermute(value, "tile", [(source_of(t), t) for t in range(count)])


def body(coil_data, frame_of, basis, sample_pos, window_at, live_count):
    parts = coil_data.shape[2]
    tiles = coil_data.shape[3]
    slots = coil_data.shape[4]
    pair = coil_data.shape[5]
    samples = coil_data.shape[6]
    coils = pair // 2
    ranks = basis.shape[1]
    tile_rows = PLANE // tiles
    devices = parts * tiles
    count = devices * slots
    depth = count * WIN_ROWS
    ys = PLANE // tiles
    my_tile = lax.axis_index("tile")
    odd = my_tile % 2

    packed = pack_slots(coil_data, frame_of, basis)
    raw = lax.all_to_all(packed, ("kz", "tile"), split_axis=0, concat_axis=0, tiled=True)

    counts = live_count.reshape(devices)
    slot_idx = jnp.arange(slots, dtype=jnp.int32)
    alive = (slot_idx[None, :] < counts[:, None]).reshape(count, 1, 1)
    pos = jnp.where(alive, sample_pos.reshape(count, 2, samples), FAR_OFF)
    row_k = taper(jnp.arange(WIN_ROWS, dtype=jnp.float32)[None, :, None] - pos[:, 0:1, :])
    col_k = taper(jnp.arange(WIN_COLS, dtype=jnp.float32)[None, :, None] - pos[:, 1:2, :])
    weights = row_k[:, :, None, :] * col_k[:, None, :, :]
    weights = weights.reshape(count, WIN_ROWS * WIN_COLS, samples).astype(jnp.bfloat16)
    corners = window_at.reshape(count, 2)
    win_row = jnp.arange(WIN_ROWS, dtype=jnp.int32)
    from_row = (2 + corners[None, :, 0] + win_row[:, None]).reshape(1, depth)
    col0 = jnp.tile(corners[:, 1], WIN_ROWS).reshape(1, depth)
    place = jnp.concatenate([from_row, col0 // COL_STEP, col0 % COL_STEP], axis=0).astype(jnp.float32)
    place = jnp.pad(place, ((ROW_NOTE, NOTES - ROW_NOTE - 3), (0, 0)))

    cos_tab, sin_tab = wave_tables()
    wave = jnp.asarray(np.concatenate([cos_tab, sin_tab], axis=1))
    wave_rows = lax.dynamic_slice_in_dim(wave, my_tile * ys, ys, 0)
    layout, span = pack_tiles(tiles, tile_rows)
    arrival, window_row = (jnp.asarray(part) for part in kx_of_lanes(layout, span))
    lane_tile = (arrival // 2 ^ my_tile // 2) * 2 + arrival % 2
    lane_rows = jnp.where(arrival < 0, -1, (lane_tile * tile_rows - 2 + window_row + PLANE) % PLANE)
    table, waves = make_tables(wave, wave_rows, lane_rows, coils)

    raw, weights, place, table, waves = lax.optimization_barrier((raw, weights, place, table, waves))
    windows = grid_windows(raw, weights, place, slots, pair)

    pairs = tiles // 2
    mine, other = [windows], []
    for hop in range(1, pairs):
        near = hop & -hop
        mine.append(from_tiles(mine[hop - near], lambda t, near=near: (t // 2 ^ near) * 2 + t % 2))
    for hop in range(pairs):
        other.append(from_tiles(mine[hop], lambda t: t // 2 * 2 + 1 - t % 2))
    odd_ref = odd.astype(jnp.int32).reshape(1)
    mids, notes = [], []
    for hop in range(pairs):
        mid, note = transform_columns(odd_ref, mine[hop], other[hop], table, wave_rows, depth, coils)
        mids.append(mid)
        notes.append(note)

    direct, mirrored = [], []
    for n, members in enumerate(layout):
        for mirror, blocks in ((None, direct), (float(tile_rows + WIN_ROWS), mirrored)):
            met = [(t if mirror is None else t ^ (tiles - 1), seat) for t, seat in members]
            block = expand_rows(
                [mids[t // 2] for t, _ in met],
                [notes[t // 2] for t, _ in met],
                [t % 2 for t, _ in met],
                [float(seat) for _, seat in met],
                n % 2,
                mirror,
                ranks,
                coils,
            ) if met else jnp.zeros_like(blocks[0])
            blocks.append(block)
    return form_image(direct, mirrored, waves)[None]


def solution(mesh):
    return jax.shard_map(
        body,
        mesh=mesh,
        in_specs=(
            P("kz", "tile", None, None, None, None, None),
            P("kz", "tile", None, None, None),
            P(),
            P("kz", "tile", None, None, None, None, None),
            P("kz", "tile", None, None, None, None),
            P("kz", "tile", None, None),
        ),
        out_specs=P("kz", None, "tile"),
        check_vma=False,
    )
```

```python
import functools
import math

import jax
import jax.numpy as jnp
import numpy as np
from jax import lax
from jax.experimental import pallas as pl
from jax.experimental.pallas import tpu as pltpu
from jax.sharding import PartitionSpec as P


PLANE = 640
WIN_ROWS = 4
WIN_COLS = 32
LANES = 128
NOTES = 16
ROW_NOTE = 13
COL_HIGH = 14
COL_LOW = 15
COL_STEP = 32
FAR_OFF = -1000.0
CHUNK = 256
NT_DIMS = (((1,), (1,)), ((), ()))


def taper(dist):
    inner = 1.0 - (dist / 1.5) ** 2
    return jnp.maximum(inner, 0.0) ** 2


def wave_tables():
    idx = np.arange(PLANE)
    phase = (idx[:, None] * idx[None, :] % PLANE) * (2.0 * math.pi / PLANE)
    return np.cos(phase).astype(jnp.bfloat16), np.sin(phase).astype(jnp.bfloat16)


def dot_nt(left, right):
    return lax.dot_general(left, right, NT_DIMS, preferred_element_type=jnp.float32)


def unit(shape, dtype=jnp.bfloat16):
    return (lax.broadcasted_iota(jnp.int32, shape, 0) == lax.broadcasted_iota(jnp.int32, shape, 1)).astype(jnp.float32).astype(dtype)


def table_kernel(coils, wave_ref, rows_ref, lanes_ref, out_ref, waves_ref):
    ys = rows_ref.shape[0]
    plane = wave_ref.shape[0]
    rows, width = out_ref.shape
    spot = lax.broadcasted_iota(jnp.int32, (LANES, width), 0)
    lane = lax.broadcasted_iota(jnp.int32, (LANES, width), 1)
    pick = (spot == lane % WIN_COLS).astype(jnp.float32).astype(jnp.bfloat16)
    cos_y = jnp.dot(rows_ref[:, :LANES], pick, preferred_element_type=jnp.float32)
    sin_y = jnp.dot(rows_ref[:, plane : plane + LANES], pick, preferred_element_type=jnp.float32)
    lane = lax.broadcasted_iota(jnp.int32, (ys, width), 1) // WIN_COLS
    into_re = jnp.where(lane < coils, cos_y, -sin_y)
    into_im = jnp.where(lane < coils, sin_y, cos_y)
    both = jnp.concatenate([into_re[:, None, None, :], into_im[:, None, None, :]], axis=1)
    both = jnp.broadcast_to(both, (ys, 2, coils, width))
    mine = lax.broadcasted_iota(jnp.int32, both.shape, 2)
    other = lax.broadcasted_iota(jnp.int32, both.shape, 3) // WIN_COLS % coils
    out_ref[...] = jnp.where(mine == other, both, 0.0).reshape(rows, width).astype(jnp.bfloat16)

    half, double = waves_ref.shape[1:]
    held = double // 2
    row = lax.broadcasted_iota(jnp.int32, (plane, held), 0)
    for parity in range(2):
        pick = (row == lanes_ref[parity : parity + 1, :]).astype(jnp.float32).astype(jnp.bfloat16)
        for part in range(2):
            waves_ref[parity, :, part * held : (part + 1) * held] = jnp.dot(
                wave_ref[:half, part * plane : (part + 1) * plane], pick, preferred_element_type=jnp.float32
            ).astype(jnp.bfloat16)


def make_tables(wave, wave_rows, lane_rows, coils):
    ys = wave_rows.shape[0]
    plane = wave.shape[0]
    return pl.pallas_call(
        functools.partial(table_kernel, coils),
        out_shape=[
            jax.ShapeDtypeStruct((ys * 2 * coils, WIN_COLS * 2 * coils), jnp.bfloat16),
            jax.ShapeDtypeStruct((2, plane // 2, 2 * lane_rows.shape[1]), jnp.bfloat16),
        ],
        compiler_params=pltpu.CompilerParams(vmem_limit_bytes=10 << 20),
        name="make_tables",
    )(wave, wave_rows, lane_rows)


def pack_kernel(frame_ref, data_ref, basis_ref, out_ref, rows_ref, rates_ref):
    parts, tiles, slots, pair, samples = data_ref.shape[2:]
    devices = parts * tiles
    rows_ref[...] = lax.dot_general(
        basis_ref[...], unit((basis_ref.shape[0], samples)), (((0,), (0,)), ((), ())), preferred_element_type=jnp.float32
    )
    out_ref[:, : slots * pair, :] = data_ref[...].reshape(devices, slots * pair, samples)
    rates_ref[...] = jnp.zeros_like(rates_ref)

    @pl.loop(0, parts)
    def _(part):
        for tile in range(tiles):
            for slot in range(slots):
                frame = frame_ref[0, 0, part, slot, tile]
                row = (part * tiles + tile) * (slots * WIN_ROWS) + slot * WIN_ROWS
                rates_ref[pl.ds(row, 1), :] = rows_ref[pl.ds(frame, 1), :]

    out_ref[:, slots * pair :, :] = rates_ref[...].reshape(devices, slots * WIN_ROWS, samples).astype(jnp.bfloat16)


def pack_slots(coil_data, frame_of, basis):
    parts, tiles, slots, pair, samples = coil_data.shape[2:]
    devices = parts * tiles
    return pl.pallas_call(
        pack_kernel,
        in_specs=[
            pl.BlockSpec(memory_space=pltpu.SMEM),
            pl.BlockSpec(memory_space=pltpu.VMEM),
            pl.BlockSpec(memory_space=pltpu.VMEM),
        ],
        out_shape=jax.ShapeDtypeStruct((devices, slots * (pair + WIN_ROWS), samples), jnp.bfloat16),
        scratch_shapes=[
            pltpu.VMEM((basis.shape[0], samples), jnp.float32),
            pltpu.VMEM((devices * slots * WIN_ROWS, samples), jnp.float32),
        ],
        compiler_params=pltpu.CompilerParams(vmem_limit_bytes=60 << 20),
        name="pack_slots",
    )(jnp.swapaxes(frame_of, 3, 4), coil_data, basis.T)


def window_kernel(slots, pair, data_ref, rate_ref, weight_ref, place_ref, out_ref, held, rates):
    sources = data_ref.shape[0]
    count = held.shape[0] // pair
    step = pl.program_id(0)
    for q in range(sources * slots):
        data = data_ref[q // slots, (q % slots) * pair : (q % slots + 1) * pair]
        first = (step * sources * slots + q) * pair
        held[pl.ds(pl.multiple_of(first, pair), pair), :] = dot_nt(data, weight_ref[q])

    @pl.when(step == pl.num_programs(0) - 1)
    def _():
        depth = place_ref.shape[1]
        width = out_ref.shape[1]
        per = LANES // WIN_COLS
        lane = lax.broadcasted_iota(jnp.int32, (count, LANES), 1) // WIN_COLS
        for group in range(pair // per):
            rows = [held[pl.ds(group * per + q, count, stride=pair), :] for q in range(per)]
            for i in range(WIN_ROWS):
                total = None
                for q in range(per):
                    turn = (q - i) % per * WIN_COLS
                    moved = pltpu.roll(rows[q], turn, 1) if turn else rows[q]
                    total = moved if total is None else jnp.where(lane == q, moved, total)
                out_ref[i * count : (i + 1) * count, group * LANES : (group + 1) * LANES] = total.astype(jnp.bfloat16)
        rates[...] = rate_ref[...].astype(jnp.float32).reshape(rates.shape)
        once = rates[pl.ds(0, count, stride=WIN_ROWS), :].astype(jnp.bfloat16)
        notes = dot_nt(unit((NOTES, LANES)), jnp.concatenate([once] * WIN_ROWS, axis=0)) + place_ref[...]
        lanes = min(depth, width)
        for part in range(depth // lanes):
            part_rows = notes[:, part * lanes : (part + 1) * lanes]
            if lanes < width:
                part_rows = jnp.concatenate([part_rows, jnp.zeros((NOTES, width - lanes), jnp.float32)], axis=1)
            out_ref[depth + part * NOTES : depth + (part + 1) * NOTES, :] = part_rows.astype(jnp.bfloat16)


def grid_windows(raw, weights, place, slots, pair):
    devices, _, samples = raw.shape
    count = devices * slots
    depth = count * WIN_ROWS
    width = WIN_COLS * pair
    sources = 8
    rate_rows = slots * WIN_ROWS
    total_rows = depth + NOTES * (depth // min(depth, width))
    return pl.pallas_call(
        functools.partial(window_kernel, slots, pair),
        grid=(devices // sources,),
        in_specs=[
            pl.BlockSpec((sources, slots * pair, samples), lambda s: (s, 0, 0)),
            pl.BlockSpec((devices, rate_rows, samples), lambda s: (0, slots * pair // rate_rows, 0)),
            pl.BlockSpec((sources * slots, LANES, samples), lambda s: (s, 0, 0)),
            pl.BlockSpec((NOTES, depth), lambda s: (0, 0)),
        ],
        out_specs=pl.BlockSpec((total_rows, width), lambda s: (0, 0)),
        out_shape=jax.ShapeDtypeStruct((total_rows, width), jnp.bfloat16),
        scratch_shapes=[
            pltpu.VMEM((count * pair, LANES), jnp.float32),
            pltpu.VMEM((devices * rate_rows, LANES), jnp.float32),
        ],
        compiler_params=pltpu.CompilerParams(vmem_limit_bytes=12 << 20),
        name="grid_windows",
    )(raw, raw, weights, place)


def columns_kernel(coils, odd_ref, mine_ref, mine_notes, other_ref, other_notes, table_ref, wave_ref, out_ref, notes_ref):
    rows = table_ref.shape[0]
    ys = rows // (2 * coils)
    plane = wave_ref.shape[1] // 2
    depth = mine_ref.shape[0]
    take_mine = odd_ref[0] == pl.program_id(0)
    grids = jnp.where(take_mine, mine_ref[...], other_ref[...])
    notes = jnp.where(take_mine, mine_notes[...], other_notes[...])
    notes_ref[0] = notes
    notes = notes.astype(jnp.float32)
    col0 = notes[COL_HIGH : COL_HIGH + 1] * COL_STEP + notes[COL_LOW : COL_LOW + 1]
    row = lax.broadcasted_iota(jnp.int32, (plane, depth), 0).astype(jnp.float32)
    corner = (row == col0).astype(jnp.float32).astype(jnp.bfloat16)
    turn_re = jnp.dot(wave_ref[:, :plane], corner, preferred_element_type=jnp.float32)[:, None, :]
    turn_im = jnp.dot(wave_ref[:, plane:], corner, preferred_element_type=jnp.float32)[:, None, :]
    flat = dot_nt(table_ref[...], grids).reshape(ys, 2, coils, depth)
    real, imag = flat[:, 0], flat[:, 1]
    done_re = real * turn_re - imag * turn_im
    done_im = real * turn_im + imag * turn_re
    both = jnp.concatenate([done_re[:, None], done_im[:, None]], axis=1)
    out_ref[0] = both.reshape(rows, depth).astype(jnp.bfloat16)


def transform_columns(odd, mine, other, table, wave_rows, depth, coils):
    width = mine.shape[1]
    rows = table.shape[0]
    ys, waves = wave_rows.shape
    chunk = min(depth, CHUNK)
    per = depth // chunk
    grid_spec = pl.BlockSpec((chunk, width), lambda e, k: (k, 0))
    note_spec = pl.BlockSpec(
        (NOTES, chunk), lambda e, k: (depth // NOTES + k * chunk // width, k * chunk % width // chunk)
    )
    return pl.pallas_call(
        functools.partial(columns_kernel, coils),
        grid=(2, per),
        in_specs=[
            pl.BlockSpec(memory_space=pltpu.SMEM),
            grid_spec,
            note_spec,
            grid_spec,
            note_spec,
            pl.BlockSpec((rows, width), lambda e, k: (0, 0)),
            pl.BlockSpec((ys, waves), lambda e, k: (0, 0)),
        ],
        out_specs=[
            pl.BlockSpec((1, rows, chunk), lambda e, k: (e, 0, k)),
            pl.BlockSpec((1, NOTES, chunk), lambda e, k: (e, 0, k)),
        ],
        out_shape=[
            jax.ShapeDtypeStruct((2, rows, depth), jnp.bfloat16),
            jax.ShapeDtypeStruct((2, NOTES, depth), jnp.bfloat16),
        ],
        compiler_params=pltpu.CompilerParams(vmem_limit_bytes=10 << 20),
        cost_estimate=pl.CostEstimate(
            flops=2 * 2 * rows * width * depth, bytes_accessed=2 * 2 * rows * depth, transcendentals=0
        ),
        name="transform_columns",
    )(odd, mine, mine, other, other, table, wave_rows)


def rows_kernel(blocks, mirror, ranks, coils, *refs):
    spread = 1 + max(group for members in blocks for group, _, _ in members)
    mids, notes, refs = refs[:spread], refs[spread : 2 * spread], refs[2 * spread :]
    earlier, refs = (refs[:2], refs[2:]) if mirror is not None else ((), refs)
    outs, held = (refs[:-1], refs[-1]) if len(refs) % 2 else (refs, None)
    _, rows, chunk = mids[0].shape
    groups = rows // coils
    step = pl.program_id(0)
    half = LANES // 2
    lane = lax.broadcasted_iota(jnp.int32, (LANES, chunk), 0)
    lefts, hits, told = [], [], []
    for second, members in enumerate(blocks):
        lefts.append(jnp.concatenate([mids[group][e] for group, e, _ in members], axis=1))
        told.append([notes[group][e].astype(jnp.float32) for group, e, _ in members])
        odd = (lane >= half) if not second else (lane < half)
        spot = (2 * (lane % half) + odd.astype(jnp.int32)).astype(jnp.float32)
        at = [note[ROW_NOTE : ROW_NOTE + 1] for note in told[second]]
        at = at if mirror is None else [mirror - row for row in at]
        hits.append([row + 2.0 * seat == spot for row, (_, _, seat) in zip(at, members)])

    def finish(pair, first, second):
        lower = lax.broadcasted_iota(jnp.int32, (rows, LANES), 1) < half
        done = []
        for a, b in ((first, second), (second, first)):
            sides = [
                jnp.where(lower, a[:, side * LANES : (side + 1) * LANES], b[:, side * LANES : (side + 1) * LANES])
                for side in range(2)
            ]
            sides = [side.reshape(groups, 1, coils, LANES) for side in sides]
            done.append(jnp.concatenate(sides, axis=1).reshape(groups, 2 * coils, LANES))
        for parity, block in enumerate(done):
            if mirror is None:
                outs[parity][:, pair] = block.astype(jnp.bfloat16)
            else:
                ahead = earlier[parity][:, pair].astype(jnp.float32)
                outs[parity][:, pair] = (ahead + block).astype(jnp.bfloat16)
                gap = (ahead - block).reshape(groups // 2, 2, 2 * coils, LANES)
                gap = jnp.concatenate([-gap[:, 1:2], gap[:, 0:1]], axis=1)
                outs[2 + parity][:, pair] = gap.reshape(groups, 2 * coils, LANES).astype(jnp.bfloat16)

    for pair in range(ranks // 2):
        totals = []
        for left, hit, note in zip(lefts, hits, told):
            right = [
                jnp.concatenate(
                    [jnp.where(h, n[rank : rank + 1], 0.0).astype(jnp.bfloat16) for h, n in zip(hit, note)], axis=1
                )
                for rank in (2 * pair, 2 * pair + 1)
            ]
            totals.append(dot_nt(left, jnp.concatenate(right, axis=0)))
        if held is None:
            finish(pair, *totals)
        else:

            @pl.when(step == 0)
            def _(pair=pair, totals=totals):
                for n in range(2):
                    held[pair, n] = totals[n]

            @pl.when(step > 0)
            def _(pair=pair, totals=totals):
                for n in range(2):
                    held[pair, n] += totals[n]

            @pl.when(step == pl.num_programs(0) - 1)
            def _(pair=pair):
                finish(pair, held[pair, 0], held[pair, 1])


def expand_rows(mids, notes, blocks, mirror, earlier, ranks, coils):
    _, rows, depth = mids[0].shape
    chunk = min(depth, CHUNK)
    per = depth // chunk
    shape = (rows // coils, ranks // 2, 2 * coils, LANES)
    outs = 2 if mirror is None else 4
    met = sum(len(members) for members in blocks)
    once = pl.BlockSpec(shape, lambda k: (0, 0, 0, 0), pipeline_mode=pl.Buffered(1))
    return pl.pallas_call(
        functools.partial(rows_kernel, blocks, mirror, ranks, coils),
        grid=(per,),
        in_specs=[
            *(pl.BlockSpec((2, rows, chunk), lambda k: (0, 0, k)) for _ in mids),
            *(pl.BlockSpec((2, NOTES, chunk), lambda k: (0, 0, k)) for _ in notes),
            *(once for _ in earlier),
        ],
        out_specs=[once] * outs,
        out_shape=[jax.ShapeDtypeStruct(shape, jnp.bfloat16)] * outs,
        scratch_shapes=[pltpu.VMEM((ranks // 2, 2, rows, 2 * LANES), jnp.float32)] if per > 1 else [],
        compiler_params=pltpu.CompilerParams(vmem_limit_bytes=10 << 20),
        cost_estimate=pl.CostEstimate(
            flops=2 * rows * met * depth * ranks * LANES, bytes_accessed=4 * rows * ranks * LANES, transcendentals=0
        ),
        name="expand_rows",
    )(*mids, *notes, *earlier)


def image_kernel(*refs):
    waves_ref, out_ref = refs[-2:]
    plane = out_ref.shape[0]
    half = plane // 2
    per = (len(refs) - 2) // 2
    groups, pairs, inner, _ = refs[0].shape
    halves = []
    for parity in range(2):
        chosen = [ref[...].reshape(groups * pairs * inner, LANES) for ref in refs[parity * per : (parity + 1) * per]]
        halves.append(dot_nt(waves_ref[parity], jnp.concatenate(chosen, axis=1)))
    out_ref[:half, :] = ((halves[0] + halves[1]) * (1.0 / plane)).astype(jnp.bfloat16)
    out_ref[half:, :] = ((halves[0] - halves[1]) * (1.0 / plane)).astype(jnp.bfloat16)


def form_image(even, odd, waves):
    plane = 2 * waves.shape[1]
    groups, pairs, inner, _ = even[0].shape
    step = next(n for n in (16, 8, 4, 2) if groups % n == 0)
    columns = step * pairs * inner
    return pl.pallas_call(
        image_kernel,
        grid=(groups // step,),
        in_specs=[
            *(pl.BlockSpec((step, pairs, inner, LANES), lambda s: (s, 0, 0, 0)) for _ in (*even, *odd)),
            pl.BlockSpec(waves.shape, lambda s: (0, 0, 0)),
        ],
        out_specs=pl.BlockSpec((plane, columns), lambda s: (0, s)),
        out_shape=jax.ShapeDtypeStruct((plane, groups * pairs * inner), jnp.bfloat16),
        compiler_params=pltpu.CompilerParams(vmem_limit_bytes=10 << 20),
        cost_estimate=pl.CostEstimate(
            flops=2 * plane * waves.shape[2] * groups * pairs * inner,
            bytes_accessed=4 * plane * groups * pairs * inner,
            transcendentals=0,
        ),
        name="form_image",
    )(*even, *odd, waves)


def pack_tiles(tiles, tile_rows):
    span = (tile_rows + WIN_ROWS) // 2 + 1
    room = LANES // 2 // span
    blocks = []
    room = min(room, tiles // 4)
    for first in range(0, tiles // 2, room):
        blocks.append([(t, n * span) for n, t in enumerate(range(first, min(first + room, tiles // 2)))])
    return blocks, span


def kx_of_lanes(blocks, span):
    half = LANES // 2
    at = np.full((2, 2, len(blocks) * half), -1, np.int32)
    for n, members in enumerate(blocks):
        for t, seat in members:
            for k in range(span):
                lane = n // 2 * LANES + seat + k
                at[:, 0, lane + half * (n % 2)] = t, 2 * k
                at[:, 1, lane + half * (1 - n % 2)] = t, 2 * k + 1
    return at


def from_tiles(value, source_of):
    count = lax.axis_size("tile")
    return lax.ppermute(value, "tile", [(source_of(t), t) for t in range(count)])


def body(coil_data, frame_of, basis, sample_pos, window_at, live_count):
    parts = coil_data.shape[2]
    tiles = coil_data.shape[3]
    slots = coil_data.shape[4]
    pair = coil_data.shape[5]
    samples = coil_data.shape[6]
    coils = pair // 2
    ranks = basis.shape[1]
    tile_rows = PLANE // tiles
    devices = parts * tiles
    count = devices * slots
    depth = count * WIN_ROWS
    ys = PLANE // tiles
    my_tile = lax.axis_index("tile")
    odd = my_tile % 2

    packed = pack_slots(coil_data, frame_of, basis)
    raw = lax.all_to_all(packed, ("kz", "tile"), split_axis=0, concat_axis=0, tiled=True)

    counts = live_count.reshape(devices)
    slot_idx = jnp.arange(slots, dtype=jnp.int32)
    alive = (slot_idx[None, :] < counts[:, None]).reshape(count, 1, 1)
    pos = jnp.where(alive, sample_pos.reshape(count, 2, samples), FAR_OFF)
    row_k = taper(jnp.arange(WIN_ROWS, dtype=jnp.float32)[None, :, None] - pos[:, 0:1, :])
    col_k = taper(jnp.arange(WIN_COLS, dtype=jnp.float32)[None, :, None] - pos[:, 1:2, :])
    weights = row_k[:, :, None, :] * col_k[:, None, :, :]
    weights = weights.reshape(count, WIN_ROWS * WIN_COLS, samples).astype(jnp.bfloat16)
    corners = window_at.reshape(count, 2)
    win_row = jnp.arange(WIN_ROWS, dtype=jnp.int32)
    from_row = (2 + corners[None, :, 0] + win_row[:, None]).reshape(1, depth)
    col0 = jnp.tile(corners[:, 1], WIN_ROWS).reshape(1, depth)
    place = jnp.concatenate([from_row, col0 // COL_STEP, col0 % COL_STEP], axis=0).astype(jnp.float32)
    place = jnp.pad(place, ((ROW_NOTE, NOTES - ROW_NOTE - 3), (0, 0)))

    cos_tab, sin_tab = wave_tables()
    wave = jnp.asarray(np.concatenate([cos_tab, sin_tab], axis=1))
    wave_rows = lax.dynamic_slice_in_dim(wave, my_tile * ys, ys, 0)
    layout, span = pack_tiles(tiles, tile_rows)
    arrival, window_row = (jnp.asarray(part) for part in kx_of_lanes(layout, span))
    lane_tile = (arrival // 2 ^ my_tile // 2) * 2 + arrival % 2
    lane_rows = jnp.where(arrival < 0, -1, (lane_tile * tile_rows - 2 + window_row + PLANE) % PLANE)
    table, waves = make_tables(wave, wave_rows, lane_rows, coils)

    raw, weights, place, table, waves = lax.optimization_barrier((raw, weights, place, table, waves))
    windows = grid_windows(raw, weights, place, slots, pair)

    pairs = tiles // 2
    mine, other = [windows], []
    for hop in range(1, pairs):
        near = hop & -hop
        mine.append(from_tiles(mine[hop - near], lambda t, near=near: (t // 2 ^ near) * 2 + t % 2))
    for hop in range(pairs):
        other.append(from_tiles(mine[hop], lambda t: t // 2 * 2 + 1 - t % 2))
    odd_ref = odd.astype(jnp.int32).reshape(1)
    mids, notes = [], []
    for hop in range(pairs):
        mid, note = transform_columns(odd_ref, mine[hop], other[hop], table, wave_rows, depth, coils)
        mids.append(mid)
        notes.append(note)

    def expand(n, mirror, earlier):
        met = [[(t if mirror is None else t ^ (tiles - 1), seat) for t, seat in members] for members in layout[n : n + 2]]
        groups = sorted({t // 2 for members in met for t, _ in members})
        blocks = [[(groups.index(t // 2), t % 2, float(seat)) for t, seat in members] for members in met]
        return expand_rows([mids[g] for g in groups], [notes[g] for g in groups], blocks, mirror, earlier, ranks, coils)

    twos = range(0, len(layout), 2)
    direct = [expand(n, None, ()) for n in twos]
    folded = [expand(n, float(tile_rows + WIN_ROWS), direct[n // 2]) for n in twos]
    even, odd_kx = ([part[2 * k + parity] for k in range(2) for part in folded] for parity in range(2))
    return form_image(even, odd_kx, waves)[None]


def solution(mesh):
    return jax.shard_map(
        body,
        mesh=mesh,
        in_specs=(
            P("kz", "tile", None, None, None, None, None),
            P("kz", "tile", None, None, None),
            P(),
            P("kz", "tile", None, None, None, None, None),
            P("kz", "tile", None, None, None, None),
            P("kz", "tile", None, None),
        ),
        out_specs=P("kz", None, "tile"),
        check_vma=False,
    )
```

```python
import functools
import math

import jax
import jax.numpy as jnp
import numpy as np
from jax import lax
from jax.experimental import pallas as pl
from jax.experimental.pallas import tpu as pltpu
from jax.sharding import PartitionSpec as P


PLANE = 640
WIN_ROWS = 4
WIN_COLS = 32
LANES = 128
NOTES = 16
ROW_NOTE = 13
COL_HIGH = 14
COL_LOW = 15
COL_STEP = 32
FAR_OFF = -1000.0
CHUNK = 256
NT_DIMS = (((1,), (1,)), ((), ()))


def taper(dist):
    inner = 1.0 - (dist / 1.5) ** 2
    return jnp.maximum(inner, 0.0) ** 2


def wave_tables():
    idx = np.arange(PLANE)
    phase = (idx[:, None] * idx[None, :] % PLANE) * (2.0 * math.pi / PLANE)
    return np.cos(phase).astype(jnp.bfloat16), np.sin(phase).astype(jnp.bfloat16)


def dot_nt(left, right):
    return lax.dot_general(left, right, NT_DIMS, preferred_element_type=jnp.float32)


def unit(shape, dtype=jnp.bfloat16):
    return (lax.broadcasted_iota(jnp.int32, shape, 0) == lax.broadcasted_iota(jnp.int32, shape, 1)).astype(jnp.float32).astype(dtype)


def table_kernel(coils, wave_ref, rows_ref, lanes_ref, out_ref, waves_ref):
    ys = rows_ref.shape[0]
    plane = wave_ref.shape[0]
    rows, width = out_ref.shape
    spot = lax.broadcasted_iota(jnp.int32, (LANES, width), 0)
    lane = lax.broadcasted_iota(jnp.int32, (LANES, width), 1)
    pick = (spot == lane % WIN_COLS).astype(jnp.float32).astype(jnp.bfloat16)
    cos_y = jnp.dot(rows_ref[:, :LANES], pick, preferred_element_type=jnp.float32)
    sin_y = jnp.dot(rows_ref[:, plane : plane + LANES], pick, preferred_element_type=jnp.float32)
    lane = lax.broadcasted_iota(jnp.int32, (ys, width), 1) // WIN_COLS
    into_re = jnp.where(lane < coils, cos_y, -sin_y)
    into_im = jnp.where(lane < coils, sin_y, cos_y)
    both = jnp.concatenate([into_re[:, None, None, :], into_im[:, None, None, :]], axis=1)
    both = jnp.broadcast_to(both, (ys, 2, coils, width))
    mine = lax.broadcasted_iota(jnp.int32, both.shape, 2)
    other = lax.broadcasted_iota(jnp.int32, both.shape, 3) // WIN_COLS % coils
    out_ref[...] = jnp.where(mine == other, both, 0.0).reshape(rows, width).astype(jnp.bfloat16)

    half, double = waves_ref.shape[1:]
    held = double // 2
    row = lax.broadcasted_iota(jnp.int32, (plane, held), 0)
    for parity in range(2):
        pick = (row == lanes_ref[parity : parity + 1, :]).astype(jnp.float32).astype(jnp.bfloat16)
        for part in range(2):
            waves_ref[parity, :, part * held : (part + 1) * held] = jnp.dot(
                wave_ref[:half, part * plane : (part + 1) * plane], pick, preferred_element_type=jnp.float32
            ).astype(jnp.bfloat16)


def make_tables(wave, wave_rows, lane_rows, coils):
    ys = wave_rows.shape[0]
    plane = wave.shape[0]
    return pl.pallas_call(
        functools.partial(table_kernel, coils),
        out_shape=[
            jax.ShapeDtypeStruct((ys * 2 * coils, WIN_COLS * 2 * coils), jnp.bfloat16),
            jax.ShapeDtypeStruct((2, plane // 2, 2 * lane_rows.shape[1]), jnp.bfloat16),
        ],
        compiler_params=pltpu.CompilerParams(vmem_limit_bytes=10 << 20),
        name="make_tables",
    )(wave, wave_rows, lane_rows)


def pack_kernel(frame_ref, data_ref, basis_ref, out_ref, rows_ref, rates_ref):
    parts, tiles, slots, pair, samples = data_ref.shape[2:]
    devices = parts * tiles
    rows_ref[...] = lax.dot_general(
        basis_ref[...], unit((basis_ref.shape[0], samples)), (((0,), (0,)), ((), ())), preferred_element_type=jnp.float32
    )
    out_ref[:, : slots * pair, :] = data_ref[...].reshape(devices, slots * pair, samples)
    rates_ref[...] = jnp.zeros_like(rates_ref)

    @pl.loop(0, parts)
    def _(part):
        for tile in range(tiles):
            for slot in range(slots):
                frame = frame_ref[0, 0, part, slot, tile]
                row = (part * tiles + tile) * (slots * WIN_ROWS) + slot * WIN_ROWS
                rates_ref[pl.ds(row, 1), :] = rows_ref[pl.ds(frame, 1), :]

    out_ref[:, slots * pair :, :] = rates_ref[...].reshape(devices, slots * WIN_ROWS, samples).astype(jnp.bfloat16)


def pack_slots(coil_data, frame_of, basis):
    parts, tiles, slots, pair, samples = coil_data.shape[2:]
    devices = parts * tiles
    return pl.pallas_call(
        pack_kernel,
        in_specs=[
            pl.BlockSpec(memory_space=pltpu.SMEM),
            pl.BlockSpec(memory_space=pltpu.VMEM),
            pl.BlockSpec(memory_space=pltpu.VMEM),
        ],
        out_shape=jax.ShapeDtypeStruct((devices, slots * (pair + WIN_ROWS), samples), jnp.bfloat16),
        scratch_shapes=[
            pltpu.VMEM((basis.shape[0], samples), jnp.float32),
            pltpu.VMEM((devices * slots * WIN_ROWS, samples), jnp.float32),
        ],
        compiler_params=pltpu.CompilerParams(vmem_limit_bytes=60 << 20),
        name="pack_slots",
    )(jnp.swapaxes(frame_of, 3, 4), coil_data, basis.T)


def window_kernel(slots, pair, data_ref, rate_ref, weight_ref, place_ref, out_ref, held, rates):
    sources = data_ref.shape[0]
    count = held.shape[0] // pair
    step = pl.program_id(0)
    for q in range(sources * slots):
        data = data_ref[q // slots, (q % slots) * pair : (q % slots + 1) * pair]
        first = (step * sources * slots + q) * pair
        held[pl.ds(pl.multiple_of(first, pair), pair), :] = dot_nt(data, weight_ref[q])

    @pl.when(step == pl.num_programs(0) - 1)
    def _():
        depth = place_ref.shape[1]
        width = out_ref.shape[1]
        per = LANES // WIN_COLS
        lane = lax.broadcasted_iota(jnp.int32, (count, LANES), 1) // WIN_COLS
        for group in range(pair // per):
            rows = [held[pl.ds(group * per + q, count, stride=pair), :] for q in range(per)]
            for i in range(WIN_ROWS):
                total = None
                for q in range(per):
                    turn = (q - i) % per * WIN_COLS
                    moved = pltpu.roll(rows[q], turn, 1) if turn else rows[q]
                    total = moved if total is None else jnp.where(lane == q, moved, total)
                out_ref[i * count : (i + 1) * count, group * LANES : (group + 1) * LANES] = total.astype(jnp.bfloat16)
        rates[...] = rate_ref[...].astype(jnp.float32).reshape(rates.shape)
        once = rates[pl.ds(0, count, stride=WIN_ROWS), :].astype(jnp.bfloat16)
        notes = dot_nt(unit((NOTES, LANES)), jnp.concatenate([once] * WIN_ROWS, axis=0)) + place_ref[...]
        lanes = min(depth, width)
        for part in range(depth // lanes):
            part_rows = notes[:, part * lanes : (part + 1) * lanes]
            if lanes < width:
                part_rows = jnp.concatenate([part_rows, jnp.zeros((NOTES, width - lanes), jnp.float32)], axis=1)
            out_ref[depth + part * NOTES : depth + (part + 1) * NOTES, :] = part_rows.astype(jnp.bfloat16)


def grid_windows(raw, weights, place, slots, pair):
    devices, _, samples = raw.shape
    count = devices * slots
    depth = count * WIN_ROWS
    width = WIN_COLS * pair
    sources = 16
    rate_rows = slots * WIN_ROWS
    total_rows = depth + NOTES * (depth // min(depth, width))
    return pl.pallas_call(
        functools.partial(window_kernel, slots, pair),
        grid=(devices // sources,),
        in_specs=[
            pl.BlockSpec((sources, slots * pair, samples), lambda s: (s, 0, 0)),
            pl.BlockSpec((devices, rate_rows, samples), lambda s: (0, slots * pair // rate_rows, 0)),
            pl.BlockSpec((sources * slots, LANES, samples), lambda s: (s, 0, 0)),
            pl.BlockSpec((NOTES, depth), lambda s: (0, 0)),
        ],
        out_specs=pl.BlockSpec((total_rows, width), lambda s: (0, 0)),
        out_shape=jax.ShapeDtypeStruct((total_rows, width), jnp.bfloat16),
        scratch_shapes=[
            pltpu.VMEM((count * pair, LANES), jnp.float32),
            pltpu.VMEM((devices * rate_rows, LANES), jnp.float32),
        ],
        compiler_params=pltpu.CompilerParams(vmem_limit_bytes=12 << 20),
        name="grid_windows",
    )(raw, raw, weights, place)


def columns_kernel(coils, odd_ref, mine_ref, mine_notes, other_ref, other_notes, table_ref, wave_ref, out_ref, notes_ref):
    rows = table_ref.shape[0]
    ys = rows // (2 * coils)
    plane = wave_ref.shape[1] // 2
    depth = mine_ref.shape[0]
    take_mine = odd_ref[0] == pl.program_id(0)
    grids = jnp.where(take_mine, mine_ref[...], other_ref[...])
    notes = jnp.where(take_mine, mine_notes[...], other_notes[...])
    notes_ref[0] = notes
    notes = notes.astype(jnp.float32)
    col0 = notes[COL_HIGH : COL_HIGH + 1] * COL_STEP + notes[COL_LOW : COL_LOW + 1]
    row = lax.broadcasted_iota(jnp.int32, (plane, depth), 0).astype(jnp.float32)
    corner = (row == col0).astype(jnp.float32).astype(jnp.bfloat16)
    turn_re = jnp.dot(wave_ref[:, :plane], corner, preferred_element_type=jnp.float32)[:, None, :]
    turn_im = jnp.dot(wave_ref[:, plane:], corner, preferred_element_type=jnp.float32)[:, None, :]
    flat = dot_nt(table_ref[...], grids).reshape(ys, 2, coils, depth)
    real, imag = flat[:, 0], flat[:, 1]
    done_re = real * turn_re - imag * turn_im
    done_im = real * turn_im + imag * turn_re
    both = jnp.concatenate([done_re[:, None], done_im[:, None]], axis=1)
    out_ref[0] = both.reshape(rows, depth).astype(jnp.bfloat16)


def transform_columns(odd, mine, other, table, wave_rows, depth, coils):
    width = mine.shape[1]
    rows = table.shape[0]
    ys, waves = wave_rows.shape
    chunk = min(depth, CHUNK)
    per = depth // chunk
    grid_spec = pl.BlockSpec((chunk, width), lambda e, k: (k, 0))
    note_spec = pl.BlockSpec(
        (NOTES, chunk), lambda e, k: (depth // NOTES + k * chunk // width, k * chunk % width // chunk)
    )
    return pl.pallas_call(
        functools.partial(columns_kernel, coils),
        grid=(2, per),
        in_specs=[
            pl.BlockSpec(memory_space=pltpu.SMEM),
            grid_spec,
            note_spec,
            grid_spec,
            note_spec,
            pl.BlockSpec((rows, width), lambda e, k: (0, 0)),
            pl.BlockSpec((ys, waves), lambda e, k: (0, 0)),
        ],
        out_specs=[
            pl.BlockSpec((1, rows, chunk), lambda e, k: (e, 0, k)),
            pl.BlockSpec((1, NOTES, chunk), lambda e, k: (e, 0, k)),
        ],
        out_shape=[
            jax.ShapeDtypeStruct((2, rows, depth), jnp.bfloat16),
            jax.ShapeDtypeStruct((2, NOTES, depth), jnp.bfloat16),
        ],
        compiler_params=pltpu.CompilerParams(vmem_limit_bytes=10 << 20),
        cost_estimate=pl.CostEstimate(
            flops=2 * 2 * rows * width * depth, bytes_accessed=2 * 2 * rows * depth, transcendentals=0
        ),
        name="transform_columns",
    )(odd, mine, mine, other, other, table, wave_rows)


def rows_kernel(blocks, mirror, ranks, coils, *refs):
    spread = 1 + max(group for members in blocks for group, _, _ in members)
    mids, notes, refs = refs[:spread], refs[spread : 2 * spread], refs[2 * spread :]
    earlier, refs = (refs[:2], refs[2:]) if mirror is not None else ((), refs)
    outs, held = (refs[:-1], refs[-1]) if len(refs) % 2 else (refs, None)
    _, rows, chunk = mids[0].shape
    groups = rows // coils
    step = pl.program_id(0)
    half = LANES // 2
    lane = lax.broadcasted_iota(jnp.int32, (LANES, chunk), 0)
    lefts, hits, told = [], [], []
    for second, members in enumerate(blocks):
        lefts.append(jnp.concatenate([mids[group][e] for group, e, _ in members], axis=1))
        told.append([notes[group][e].astype(jnp.float32) for group, e, _ in members])
        odd = (lane >= half) if not second else (lane < half)
        spot = (2 * (lane % half) + odd.astype(jnp.int32)).astype(jnp.float32)
        at = [note[ROW_NOTE : ROW_NOTE + 1] for note in told[second]]
        at = at if mirror is None else [mirror - row for row in at]
        hits.append([row + 2.0 * seat == spot for row, (_, _, seat) in zip(at, members)])

    def finish(pair, first, second):
        lower = lax.broadcasted_iota(jnp.int32, (rows, LANES), 1) < half
        done = []
        for a, b in ((first, second), (second, first)):
            sides = [
                jnp.where(lower, a[:, side * LANES : (side + 1) * LANES], b[:, side * LANES : (side + 1) * LANES])
                for side in range(2)
            ]
            sides = [side.reshape(groups, 1, coils, LANES) for side in sides]
            done.append(jnp.concatenate(sides, axis=1).reshape(groups, 2 * coils, LANES))
        for parity, block in enumerate(done):
            if mirror is None:
                outs[parity][:, pair] = block.astype(jnp.bfloat16)
            else:
                ahead = earlier[parity][:, pair].astype(jnp.float32)
                outs[parity][:, pair] = (ahead + block).astype(jnp.bfloat16)
                gap = (ahead - block).reshape(groups // 2, 2, 2 * coils, LANES)
                gap = jnp.concatenate([-gap[:, 1:2], gap[:, 0:1]], axis=1)
                outs[2 + parity][:, pair] = gap.reshape(groups, 2 * coils, LANES).astype(jnp.bfloat16)

    for pair in range(ranks // 2):
        totals = []
        for left, hit, note in zip(lefts, hits, told):
            right = [
                jnp.concatenate(
                    [jnp.where(h, n[rank : rank + 1], 0.0).astype(jnp.bfloat16) for h, n in zip(hit, note)], axis=1
                )
                for rank in (2 * pair, 2 * pair + 1)
            ]
            totals.append(dot_nt(left, jnp.concatenate(right, axis=0)))
        if held is None:
            finish(pair, *totals)
        else:

            @pl.when(step == 0)
            def _(pair=pair, totals=totals):
                for n in range(2):
                    held[pair, n] = totals[n]

            @pl.when(step > 0)
            def _(pair=pair, totals=totals):
                for n in range(2):
                    held[pair, n] += totals[n]

            @pl.when(step == pl.num_programs(0) - 1)
            def _(pair=pair):
                finish(pair, held[pair, 0], held[pair, 1])


def expand_rows(mids, notes, blocks, mirror, earlier, ranks, coils):
    _, rows, depth = mids[0].shape
    chunk = min(depth, CHUNK)
    per = depth // chunk
    shape = (rows // coils, ranks // 2, 2 * coils, LANES)
    outs = 2 if mirror is None else 4
    met = sum(len(members) for members in blocks)
    once = pl.BlockSpec(shape, lambda k: (0, 0, 0, 0), pipeline_mode=pl.Buffered(1))
    return pl.pallas_call(
        functools.partial(rows_kernel, blocks, mirror, ranks, coils),
        grid=(per,),
        in_specs=[
            *(pl.BlockSpec((2, rows, chunk), lambda k: (0, 0, k)) for _ in mids),
            *(pl.BlockSpec((2, NOTES, chunk), lambda k: (0, 0, k)) for _ in notes),
            *(once for _ in earlier),
        ],
        out_specs=[once] * outs,
        out_shape=[jax.ShapeDtypeStruct(shape, jnp.bfloat16)] * outs,
        scratch_shapes=[pltpu.VMEM((ranks // 2, 2, rows, 2 * LANES), jnp.float32)] if per > 1 else [],
        compiler_params=pltpu.CompilerParams(vmem_limit_bytes=10 << 20),
        cost_estimate=pl.CostEstimate(
            flops=2 * rows * met * depth * ranks * LANES, bytes_accessed=4 * rows * ranks * LANES, transcendentals=0
        ),
        name="expand_rows",
    )(*mids, *notes, *earlier)


def image_kernel(*refs):
    waves_ref, out_ref = refs[-2:]
    plane = out_ref.shape[0]
    half = plane // 2
    per = (len(refs) - 2) // 2
    groups, pairs, inner, _ = refs[0].shape
    halves = []
    for parity in range(2):
        chosen = [ref[...].reshape(groups * pairs * inner, LANES) for ref in refs[parity * per : (parity + 1) * per]]
        halves.append(dot_nt(waves_ref[parity], jnp.concatenate(chosen, axis=1)))
    out_ref[:half, :] = ((halves[0] + halves[1]) * (1.0 / plane)).astype(jnp.bfloat16)
    out_ref[half:, :] = ((halves[0] - halves[1]) * (1.0 / plane)).astype(jnp.bfloat16)


def form_image(even, odd, waves):
    plane = 2 * waves.shape[1]
    groups, pairs, inner, _ = even[0].shape
    step = next(n for n in (32, 16, 8, 4, 2) if groups % n == 0)
    columns = step * pairs * inner
    return pl.pallas_call(
        image_kernel,
        grid=(groups // step,),
        in_specs=[
            *(pl.BlockSpec((step, pairs, inner, LANES), lambda s: (s, 0, 0, 0)) for _ in (*even, *odd)),
            pl.BlockSpec(waves.shape, lambda s: (0, 0, 0)),
        ],
        out_specs=pl.BlockSpec((plane, columns), lambda s: (0, s)),
        out_shape=jax.ShapeDtypeStruct((plane, groups * pairs * inner), jnp.bfloat16),
        compiler_params=pltpu.CompilerParams(vmem_limit_bytes=20 << 20),
        cost_estimate=pl.CostEstimate(
            flops=2 * plane * waves.shape[2] * groups * pairs * inner,
            bytes_accessed=4 * plane * groups * pairs * inner,
            transcendentals=0,
        ),
        name="form_image",
    )(*even, *odd, waves)


def pack_tiles(tiles, tile_rows):
    span = (tile_rows + WIN_ROWS) // 2 + 1
    room = LANES // 2 // span
    blocks = []
    room = min(room, tiles // 4)
    for first in range(0, tiles // 2, room):
        blocks.append([(t, n * span) for n, t in enumerate(range(first, min(first + room, tiles // 2)))])
    return blocks, span


def kx_of_lanes(blocks, span):
    half = LANES // 2
    at = np.full((2, 2, len(blocks) * half), -1, np.int32)
    for n, members in enumerate(blocks):
        for t, seat in members:
            for k in range(span):
                lane = n // 2 * LANES + seat + k
                at[:, 0, lane + half * (n % 2)] = t, 2 * k
                at[:, 1, lane + half * (1 - n % 2)] = t, 2 * k + 1
    return at


def from_tiles(value, source_of):
    count = lax.axis_size("tile")
    return lax.ppermute(value, "tile", [(source_of(t), t) for t in range(count)])


def body(coil_data, frame_of, basis, sample_pos, window_at, live_count):
    parts = coil_data.shape[2]
    tiles = coil_data.shape[3]
    slots = coil_data.shape[4]
    pair = coil_data.shape[5]
    samples = coil_data.shape[6]
    coils = pair // 2
    ranks = basis.shape[1]
    tile_rows = PLANE // tiles
    devices = parts * tiles
    count = devices * slots
    depth = count * WIN_ROWS
    ys = PLANE // tiles
    my_tile = lax.axis_index("tile")
    odd = my_tile % 2

    packed = pack_slots(coil_data, frame_of, basis)
    raw = lax.all_to_all(packed, ("kz", "tile"), split_axis=0, concat_axis=0, tiled=True)

    counts = live_count.reshape(devices)
    slot_idx = jnp.arange(slots, dtype=jnp.int32)
    alive = (slot_idx[None, :] < counts[:, None]).reshape(count, 1, 1)
    pos = jnp.where(alive, sample_pos.reshape(count, 2, samples), FAR_OFF)
    row_k = taper(jnp.arange(WIN_ROWS, dtype=jnp.float32)[None, :, None] - pos[:, 0:1, :])
    col_k = taper(jnp.arange(WIN_COLS, dtype=jnp.float32)[None, :, None] - pos[:, 1:2, :])
    weights = row_k[:, :, None, :] * col_k[:, None, :, :]
    weights = weights.reshape(count, WIN_ROWS * WIN_COLS, samples).astype(jnp.bfloat16)
    corners = window_at.reshape(count, 2)
    win_row = jnp.arange(WIN_ROWS, dtype=jnp.int32)
    from_row = (2 + corners[None, :, 0] + win_row[:, None]).reshape(1, depth)
    col0 = jnp.tile(corners[:, 1], WIN_ROWS).reshape(1, depth)
    place = jnp.concatenate([from_row, col0 // COL_STEP, col0 % COL_STEP], axis=0).astype(jnp.float32)
    place = jnp.pad(place, ((ROW_NOTE, NOTES - ROW_NOTE - 3), (0, 0)))

    cos_tab, sin_tab = wave_tables()
    wave = jnp.asarray(np.concatenate([cos_tab, sin_tab], axis=1))
    wave_rows = lax.dynamic_slice_in_dim(wave, my_tile * ys, ys, 0)
    layout, span = pack_tiles(tiles, tile_rows)
    arrival, window_row = (jnp.asarray(part) for part in kx_of_lanes(layout, span))
    lane_tile = (arrival // 2 ^ my_tile // 2) * 2 + arrival % 2
    lane_rows = jnp.where(arrival < 0, -1, (lane_tile * tile_rows - 2 + window_row + PLANE) % PLANE)
    table, waves = make_tables(wave, wave_rows, lane_rows, coils)

    raw, weights, place, table, waves = lax.optimization_barrier((raw, weights, place, table, waves))
    windows = grid_windows(raw, weights, place, slots, pair)

    pairs = tiles // 2
    mine, other = [windows], []
    for hop in range(1, pairs):
        near = hop & -hop
        mine.append(from_tiles(mine[hop - near], lambda t, near=near: (t // 2 ^ near) * 2 + t % 2))
    for hop in range(pairs):
        other.append(from_tiles(mine[hop], lambda t: t // 2 * 2 + 1 - t % 2))
    odd_ref = odd.astype(jnp.int32).reshape(1)
    mids, notes = [], []
    for hop in range(pairs):
        mid, note = transform_columns(odd_ref, mine[hop], other[hop], table, wave_rows, depth, coils)
        mids.append(mid)
        notes.append(note)

    def expand(n, mirror, earlier):
        met = [[(t if mirror is None else t ^ (tiles - 1), seat) for t, seat in members] for members in layout[n : n + 2]]
        groups = sorted({t // 2 for members in met for t, _ in members})
        blocks = [[(groups.index(t // 2), t % 2, float(seat)) for t, seat in members] for members in met]
        return expand_rows([mids[g] for g in groups], [notes[g] for g in groups], blocks, mirror, earlier, ranks, coils)

    twos = range(0, len(layout), 2)
    direct = [expand(n, None, ()) for n in twos]
    folded = [expand(n, float(tile_rows + WIN_ROWS), direct[n // 2]) for n in twos]
    even, odd_kx = ([part[2 * k + parity] for k in range(2) for part in folded] for parity in range(2))
    return form_image(even, odd_kx, waves)[None]


def solution(mesh):
    return jax.shard_map(
        body,
        mesh=mesh,
        in_specs=(
            P("kz", "tile", None, None, None, None, None),
            P("kz", "tile", None, None, None),
            P(),
            P("kz", "tile", None, None, None, None, None),
            P("kz", "tile", None, None, None, None),
            P("kz", "tile", None, None),
        ),
        out_specs=P("kz", None, "tile"),
        check_vma=False,
    )
```
